256 devices in a mesh: fsdp: 16 (over y, x), ep: 16 (over z, core).
Axes of the slice: x: 4, y: 4, z: 8, core: 2. Of those that a mesh axis runs over, the one named last changes fastest.
Arguments:
- tokens: bfloat16 [8192, 7168], P('ep', 'fsdp'), may hold values from -6 to 6
- cotangent: bfloat16 [8192, 7168], P('ep', 'fsdp'), may hold values from -3 to 3
- gate_weight: bfloat16 [16, 7168, 2048], P('ep', None, 'fsdp'), may hold values from -0.0625 to 0.0625
- up_weight: bfloat16 [16, 7168, 2048], P('ep', None, 'fsdp'), may hold values from -0.0625 to 0.0625
- down_weight: bfloat16 [16, 2048, 7168], P('ep', 'fsdp'), may hold values from -0.125 to 0.125
- chosen: int32 [16, 16, 16], P(None, 'ep'), may hold values from 0 to 511, as said below
- counts: int32 [16, 16], P(None, 'ep'), may hold values from 1 to 16, as said below
- gate_prob: float32 [16, 16, 16], P(None, 'ep'), may hold values from 0.2 to 1
Outputs:
- mixture: bfloat16 [8192, 7168], P('ep', 'fsdp')
- grad_tokens: bfloat16 [8192, 7168], P('ep', 'fsdp')
- grad_gate: bfloat16 [16, 7168, 2048], P('ep', None, 'fsdp')
- grad_up: bfloat16 [16, 7168, 2048], P('ep', None, 'fsdp')
- grad_down: bfloat16 [16, 2048, 7168], P('ep', 'fsdp')
The draws below stay inside these ranges and needn't reach their ends.
Inputs may be any that keep to these rules, and one draw needn't show every extreme that they name: For each expert e and group s the entries chosen[e, s, j] with j < counts[e, s] are distinct; the remaining entries are padding. `counts`: in every draw one expert takes 16 rows from every group.
All inputs are finite; a program needn't handle non-finite values.
Results may differ from the reference program's by a relative error of at most 0.017.
Values may be sent and summed in bfloat16 or wider, within the bound.
A program may use at most 192 MiB of HBM per device.

```python
import jax
import jax.numpy as jnp
from jax import lax

D = 7168
H = 2048
TOK = 512
SLOT = 16
GROUPS = 16
EXPERTS = 16
TOKENS = 8192
N_FSDP = 16


def first_slots(subkey):
    return jax.random.permutation(subkey, TOK)[:SLOT]


def draw_chosen(key, part):
    subkeys = jax.random.split(jax.random.fold_in(key, 11), EXPERTS * GROUPS)
    picked = jax.vmap(first_slots)(subkeys)
    return picked.reshape(EXPERTS, GROUPS, SLOT).astype(jnp.int32)


def draw_counts(key, part):
    level_key, count_key, busy_key = jax.random.split(jax.random.fold_in(key, 23), 3)
    levels = jax.random.randint(level_key, (EXPERTS, 1), 1, SLOT + 1)
    lowest = jnp.maximum(levels // 2, 1)
    spread = jax.random.randint(count_key, (EXPERTS, GROUPS), 0, 1048576)
    drawn = lowest + spread % (levels - lowest + 1)
    busiest = jax.random.randint(busy_key, (1, 1), 0, EXPERTS)
    expert_ids = jnp.arange(EXPERTS)[:, None]
    return jnp.where(expert_ids == busiest, SLOT, drawn).astype(jnp.int32)


def shard_levels(stream_key, extent, shards, smallest, high):
    loudness, own = 1.0, jax.random.fold_in(stream_key, 6)
    for dim, blocks in shards:
        draws = jnp.exp(jax.random.uniform(jax.random.fold_in(own, dim), (blocks,), jnp.float32, smallest / len(shards), high / len(shards)))
        loudness = loudness * jnp.repeat(draws, extent[dim] // blocks).reshape([-1 if axis == dim else 1 for axis in range(len(extent))])
    return loudness


def bell_draw(stream_key, dims, deviation, limit, cuts=(), kind=jnp.bfloat16):
    factor_of = shard_levels(stream_key, dims, cuts, -0.22, 0.18) if cuts else 1.0
    entries = jax.random.normal(stream_key, dims, jnp.float32) * deviation * factor_of
    return jnp.minimum(jnp.maximum(entries, -limit), limit).astype(kind)


def setup_inputs(seed: int = 0) -> dict:
    streams_of = jax.random.split(jax.random.key(seed), 9)
    tokens = bell_draw(streams_of[0], (TOKENS, D), 1.0, 6.0, ((0, 16), (1, 16)))
    cotangent = bell_draw(streams_of[1], (TOKENS, D), 0.5, 3.0, ((0, 16), (1, 16)))
    gate_weight = bell_draw(streams_of[2], (EXPERTS, D, H), D ** -0.5, 0.0625, ((0, 16), (2, 16)))
    up_weight = bell_draw(streams_of[3], (EXPERTS, D, H), D ** -0.5, 0.0625, ((0, 16), (2, 16)))
    down_weight = bell_draw(streams_of[4], (EXPERTS, H, D), H ** -0.5, 0.125, ((0, 16), (1, 16)))
    chosen = draw_chosen(jax.random.fold_in(streams_of[8], 71), 0)
    counts = draw_counts(jax.random.fold_in(streams_of[8], 71), 0)
    gate_prob = jnp.clip(0.2 + 0.8 * jax.random.uniform(streams_of[7], (EXPERTS, GROUPS, SLOT), jnp.float32) ** shard_levels(streams_of[7], (EXPERTS, GROUPS, SLOT), ((1, 16),), -0.2, 0.2), 0.2, 1.0)
    return dict(tokens=tokens, cotangent=cotangent, gate_weight=gate_weight, up_weight=up_weight, down_weight=down_weight, chosen=chosen, counts=counts, gate_prob=gate_prob)


def split_hidden(matrix):
    return matrix.astype(jnp.float32).reshape(matrix.shape[0], N_FSDP, matrix.shape[1] // N_FSDP)


def rounded_total(partials):
    kept = lax.optimization_barrier(partials.astype(jnp.bfloat16))
    return jnp.sum(kept.astype(jnp.float32), axis=0)


def reference(tokens, cotangent, gate_weight, up_weight, down_weight, chosen, counts, gate_prob):
    offsets = (jnp.arange(GROUPS, dtype=jnp.int32) * TOK)[:, None]
    position = jnp.arange(SLOT, dtype=jnp.int32)[None, :]
    mixture = jnp.zeros((TOKENS, D), jnp.float32)
    grad_tokens = jnp.zeros((TOKENS, D), jnp.float32)
    gate_grads = []
    up_grads = []
    down_grads = []
    contract_rows = (((0,), (0,)), ((), ()))
    contract_last = (((1,), (1,)), ((), ()))
    for expert in range(EXPERTS):
        row_ids = (chosen[expert].astype(jnp.int32) + offsets).reshape(-1).astype(jnp.int32)
        live_mask = (position < counts[expert].astype(jnp.int32)[:, None]).reshape(-1)
        weight = jnp.where(live_mask, gate_prob[expert].reshape(-1), 0.0).astype(jnp.float32)
        gathered = tokens[row_ids]
        picked = jnp.where(live_mask[:, None], gathered, jnp.zeros_like(gathered))
        picked_grads = (weight[:, None] * cotangent[row_ids].astype(jnp.float32)).astype(jnp.bfloat16)
        pre_gate = jnp.dot(picked, gate_weight[expert], preferred_element_type=jnp.float32)
        pre_up = jnp.dot(picked, up_weight[expert], preferred_element_type=jnp.float32)
        sigmoid_gate = jax.nn.sigmoid(pre_gate)
        activated = pre_gate * sigmoid_gate
        hidden = (activated * pre_up).astype(jnp.bfloat16)
        down_blocks = down_weight[expert].astype(jnp.float32).reshape(N_FSDP, H // N_FSDP, D)
        partials = jnp.einsum("rkh,khd->krd", split_hidden(hidden), down_blocks, precision=lax.Precision.HIGHEST)
        output = rounded_total(partials).astype(jnp.bfloat16)
        mixture = mixture.at[row_ids].add(weight[:, None] * output.astype(jnp.float32))
        grad_hidden = lax.dot_general(picked_grads, down_weight[expert], contract_last, preferred_element_type=jnp.float32)
        grad_pre_gate = (grad_hidden * pre_up * sigmoid_gate * (1.0 + pre_gate * (1.0 - sigmoid_gate))).astype(jnp.bfloat16)
        grad_pre_up = (grad_hidden * activated).astype(jnp.bfloat16)
        down_grads.append(lax.dot_general(hidden, picked_grads, contract_rows, preferred_element_type=jnp.float32).astype(jnp.bfloat16))
        gate_grads.append(lax.dot_general(picked, grad_pre_gate, contract_rows, preferred_element_type=jnp.float32).astype(jnp.bfloat16))
        up_grads.append(lax.dot_general(picked, grad_pre_up, contract_rows, preferred_element_type=jnp.float32).astype(jnp.bfloat16))
        gate_blocks = gate_weight[expert].astype(jnp.float32).reshape(D, N_FSDP, H // N_FSDP)
        up_blocks = up_weight[expert].astype(jnp.float32).reshape(D, N_FSDP, H // N_FSDP)
        partials = jnp.einsum("rkh,dkh->krd", split_hidden(grad_pre_gate), gate_blocks, precision=lax.Precision.HIGHEST)
        partials = partials + jnp.einsum("rkh,dkh->krd", split_hidden(grad_pre_up), up_blocks, precision=lax.Precision.HIGHEST)
        returned = rounded_total(partials).astype(jnp.bfloat16)
        grad_tokens = grad_tokens.at[row_ids].add(jnp.where(live_mask[:, None], returned.astype(jnp.float32), 0.0))
    return (mixture.astype(jnp.bfloat16), grad_tokens.astype(jnp.bfloat16), jnp.stack(gate_grads), jnp.stack(up_grads), jnp.stack(down_grads))
```

```python
import jax
import jax.numpy as jnp
from jax import lax
from jax.experimental import pallas as pl
from jax.experimental.pallas import tpu as pltpu
from jax.sharding import PartitionSpec as P

MESH = pl.DeviceIdType.MESH
BF = jnp.bfloat16
F32 = jnp.float32
SIDE = 4
RING = (0, -1, 1, 2)
LAST = (((1,), (1,)), ((), ()))
ROWS = (((0,), (0,)), ((), ()))


def dot(a, b, dims=(((1,), (0,)), ((), ()))):
    return lax.dot_general(a, b, dims, preferred_element_type=F32)


def kernel(
    idx_ref, row_idx_ref, w_ref, tok_ref, cot_ref, gate_hbm, up_hbm, down_hbm,
    mixture_ref, grad_tok_ref, ggate_hbm, gup_hbm, gdown_hbm,
    tok_loc, grad_loc, tok_all, grad_all, tok_rem, grad_rem,
    gate, up, down, ggate, gup, gdown,
    out_part, out_rem, ret_part, pre, gh, hid, gpre,
    out_in, out_in2, ret_in, ret_in2, out_res, ret_res, out_back, ret_back,
    w_sem, a2a_send, a2a_recv, ag_send, ag_recv, rs_send, rs_recv, back_send, back_recv, gout_sem,
):
    f = lax.axis_index("fsdp")
    me = lax.axis_index("ep")
    n_ep = idx_ref.shape[0] // 16
    y = lax.div(f, SIDE)
    x = lax.rem(f, SIDE)
    odd = lax.rem(x, 2)
    wide = tok_all.shape[2]
    main = grad_all.shape[2]
    rows = tok_all.shape[1]
    half = rows // 2
    quarter = rows // 4
    feats = tok_ref.shape[1]
    pair = 2 * feats
    slot = 16

    def flat(dy, dx):
        return lax.rem(y + dy + SIDE, SIDE) * SIDE + lax.rem(x + dx + SIDE, SIDE)

    def coord(axis, along, other=0):
        return (other, along) if axis == 0 else (along, other)

    barrier = pltpu.get_barrier_semaphore()
    for dy, dx in ((0, 1), (0, -1), (1, 0), (-1, 0)):
        pl.semaphore_signal(barrier, inc=1, device_id={"fsdp": flat(dy, dx)}, device_id_type=MESH)

    @pl.loop(1, n_ep)
    def _(k):
        pl.semaphore_signal(barrier, inc=1, device_id={"ep": lax.rem(me + k, n_ep)}, device_id_type=MESH)

    loads = [
        pltpu.make_async_copy(src, dst, w_sem.at[i])
        for i, (src, dst) in enumerate(((gate_hbm, gate), (up_hbm, up), (down_hbm, down)))
    ]
    for load in loads:
        load.start()

    n_tok = tok_ref.shape[0]
    fi = lax.broadcasted_iota(jnp.int32, (feats, wide), 0)
    fj = lax.broadcasted_iota(jnp.int32, (feats, wide), 1)

    def packing(delta, low):
        body = (fi == fj + 64 * odd) & (fj < main)
        tail = (fi == fj - delta) & (fj >= low) & (fj < low + 64)
        return jnp.where(body | tail, 1.0, 0.0).astype(BF)

    pack_a = packing(448 * odd, 384 + 64 * odd)
    pack_b = packing(64 + 320 * odd, 448 - 64 * odd)
    hit = lax.broadcasted_iota(jnp.int32, (rows, n_tok), 1) == idx_ref[...]
    onehot = jnp.where(hit, 1.0, 0.0).astype(BF)
    tp = dot(dot(onehot, tok_ref[...]).astype(BF), pack_a)
    gp = dot((dot(onehot, cot_ref[...]) * w_ref[...]).astype(BF), pack_b)
    tok_loc[:, :main] = tp[:, :main].astype(BF)
    tok_loc[:, main:] = (tp[:, main:] + gp[:, main:]).astype(BF)
    grad_loc[...] = gp[:, :main].astype(BF)

    pl.semaphore_wait(barrier, n_ep + 3)

    def scatter(src, dst_of, send, recv):
        @pl.loop(1, n_ep)
        def _(k):
            peer = lax.rem(me + k, n_ep)
            pltpu.make_async_remote_copy(
                src_ref=src.at[pl.ds(peer * slot, slot)],
                dst_ref=dst_of(me * slot),
                send_sem=send,
                recv_sem=recv,
                device_id={"ep": peer},
                device_id_type=MESH,
            ).start()

        pltpu.make_async_copy(src.at[pl.ds(me * slot, slot)], dst_of(me * slot), recv).start()

    def wait_bytes(ref, sem):
        pltpu.make_async_copy(ref, ref, sem).wait()

    part = lax.div(me, n_ep // 2)
    scatter(tok_loc, lambda r: tok_all.at[f, pl.ds(r, slot)], a2a_send.at[0], a2a_recv.at[part])
    scatter(grad_loc, lambda r: grad_all.at[f, pl.ds(r, slot)], a2a_send.at[1], a2a_recv.at[2 + part])

    def put(src, dst, send, recv, axis, step):
        dy, dx = coord(axis, step)
        pltpu.make_async_remote_copy(
            src_ref=src, dst_ref=dst, send_sem=send, recv_sem=recv,
            device_id={"fsdp": flat(dy, dx)}, device_id_type=MESH,
        ).start()

    def gather(buf, which):
        send = ag_send.at[which]

        def sem(h, i):
            return ag_recv.at[which * 40 + h * 20 + i]

        def ref(h, fst, snd, q=None):
            o = coord(h, fst, snd)
            first = h * half + (0 if q is None else q * quarter)
            return buf.at[flat(*o), pl.ds(first, half if q is None else quarter)]

        def wait(h, i, fst, snd, q=None):
            wait_bytes(ref(h, fst, snd, q), sem(h, i))

        def send_block(h, i, fst, snd, axis, step, q=None):
            r = ref(h, fst, snd, q)
            put(r, r, send, sem(h, i), axis, step)

        def own(h):
            for i, step in ((0, 1), (1, -1)):
                send_block(h, i, 0, 0, h, step)
            for i, step in ((4, 1), (5, -1)):
                send_block(h, i, 0, 0, 1 - h, step)

        def spread(h, j):
            for i, step in ((0, 1), (1, -1)):
                send_block(h, 4 + 4 * j + i, RING[j], 0, 1 - h, step)

        def s1():
            for i in (0, 1):
                o = (-1, 1)[i]
                for h in (0, 1):
                    wait(h, i, o, 0)
                    send_block(h, 2 + i, o, 0, h, -o, i)
                for h in (0, 1):
                    spread(h, 1 + i)

        def relay(j):
            for i in (0, 1):
                o = (-1, 1)[i]
                for h in (1, 0):
                    wait(h, 4 + 4 * j + i, RING[j], o)
                    send_block(h, 6 + 4 * j + i, RING[j], o, 1 - h, -o, i)

        def s3():
            for h in (0, 1):
                wait(h, 2, 2, 0, 0)
                wait(h, 3, 2, 0, 1)
                spread(h, 3)

        def finish():
            for j in range(4):
                for h in (0, 1):
                    for i in (0, 1):
                        wait(h, 6 + 4 * j + i, RING[j], 2, i)

        return own, s1, relay, s3, finish

    def reduce(buf, in1, in2, res, which):
        send = rs_send.at[which]
        order = (3, 2, 1, 0)

        def sem(h, j, i):
            return rs_recv.at[which * 60 + h * 30 + j * 6 + i]

        def piece(h, fst, snd, q=None):
            o = coord(h, fst, snd)
            first = h * half + (0 if q is None else q * quarter)
            return buf.at[flat(*o), pl.ds(first, half if q is None else quarter)]

        def land(h, j, first, n):
            if j < 4:
                return in1.at[h, j, pl.ds(first, n)]
            return in2.at[h, pl.ds(first, n)]

        def term(h, j, k, q=None):
            if j < 4:
                return piece(h, RING[j], k, q)
            return piece(h, k, 0, q)

        q1, q2, fp, fm = 0, quarter, half, 2 * half

        def axis_of(h, j):
            return 1 - h if j < 4 else h

        def init(h, j):
            ax = axis_of(h, j)
            put(term(h, j, 2, 0), land(h, j, q1, quarter), send, sem(h, j, 0), ax, 1)
            put(term(h, j, 2, 1), land(h, j, q2, quarter), send, sem(h, j, 1), ax, -1)
            put(term(h, j, 1, 1), land(h, j, fp + quarter, quarter), send, sem(h, j, 2), ax, 1)
            put(term(h, j, -1, 0), land(h, j, fm, quarter), send, sem(h, j, 3), ax, -1)

        def comb(h, j):
            ax = axis_of(h, j)
            for i, k, first, dst in ((0, 1, q1, fp), (1, -1, q2, fm + quarter)):
                r = land(h, j, first, quarter)
                wait_bytes(r, sem(h, j, i))
                r[...] = (r[...].astype(F32) + term(h, j, k, i)[...].astype(F32)).astype(BF)
                put(r, land(h, j, dst, quarter), send, sem(h, j, 4 + i), ax, k)

        def fin(h, j):
            for first, i in ((fp + quarter, 2), (fm, 3), (fp, 4), (fm + quarter, 5)):
                wait_bytes(land(h, j, first, quarter), sem(h, j, i))
            own = term(h, j, 0)
            total = (
                own[...].astype(F32)
                + land(h, j, fp, half)[...].astype(F32)
                + land(h, j, fm, half)[...].astype(F32)
            ).astype(BF)
            if j < 4:
                own[...] = total
            else:
                res[pl.ds(h * half, half)] = total

        return init, comb, fin

    own, s1, relay, s3, finish = gather(tok_all, 0)
    for h in (0, 1):
        wait_bytes(tok_all.at[f, pl.ds(h * half, half)], a2a_recv.at[h])
        own(h)
    s1()
    relay(0)
    s3()
    relay(1)
    relay(2)
    relay(3)
    own2, s1b, relay2, s3b, finish2 = gather(grad_all, 1)
    for h in (0, 1):
        wait_bytes(grad_all.at[f, pl.ds(h * half, half)], a2a_recv.at[2 + h])
        own2(h)
    finish()

    n_pair = tok_all.shape[0] // 2
    low = lax.broadcasted_iota(jnp.int32, (rows, 128), 1) < 64
    for load in loads:
        load.wait()

    def span(p, size=pair):
        return pl.ds(pl.multiple_of(p * pair, 128), size)

    def tok_pair(p):
        return jnp.concatenate(
            [tok_all[2 * p, :, :main], tok_rem[p], tok_all[2 * p + 1, :, :main]], axis=1
        )

    def grad_pair(p):
        return jnp.concatenate([grad_all[2 * p], grad_rem[p], grad_all[2 * p + 1]], axis=1)

    pre[...] = jnp.zeros_like(pre)
    gh[...] = jnp.zeros_like(gh)

    @pl.loop(0, n_pair)
    def _(p):
        even = tok_all[2 * p, :, main:].astype(F32)
        other = tok_all[2 * p + 1, :, main:].astype(F32)
        tok_rem[p] = jnp.where(low, even, other).astype(BF)
        grad_rem[p] = pltpu.roll(jnp.where(low, other, even), 64, 1).astype(BF)
        both = jnp.concatenate([gate[span(p)], up[span(p)]], axis=1)
        pre[...] += dot(tok_pair(p), both)

    pg = pre[:, :128]
    pu = pre[:, 128:]
    sg = jax.nn.sigmoid(pg)
    hid[...] = (pg * sg * pu).astype(BF)
    s1b()
    relay2(0)

    @pl.loop(0, n_pair)
    def _(p):
        o = dot(hid[...], down[:, span(p)]).astype(BF)
        out_part[2 * p] = o[:, :main]
        out_rem[p] = o[:, main:wide]
        out_part[2 * p + 1] = o[:, wide:]

    s3b()
    relay2(1)
    relay2(2)
    relay2(3)
    init, comb, fin = reduce(out_part, out_in, out_in2, out_res, 0)
    for j in (3, 2, 1, 0):
        for h in (0, 1):
            init(h, j)
    finish2()

    @pl.loop(0, n_pair)
    def _(p):
        gh[...] += dot(grad_pair(p), down[:, span(p)], LAST)

    pg = pre[:, :128]
    pu = pre[:, 128:]
    sg = jax.nn.sigmoid(pg)
    gpre[:, :128] = (gh[...] * pu * sg * (1.0 + pg * (1.0 - sg))).astype(BF)
    gpre[:, 128:] = (gh[...] * (pg * sg)).astype(BF)
    for j in (3, 2):
        for h in (0, 1):
            comb(h, j)

    @pl.loop(0, n_pair)
    def _(p):
        both = jnp.concatenate([gate[span(p)], up[span(p)]], axis=1)
        r = dot(gpre[...], both, LAST)
        ret_part[2 * p, :, :main] = r[:, :main].astype(BF)
        ret_part[2 * p + 1, :, :main] = r[:, wide:].astype(BF)
        rem = pltpu.roll(r[:, main:wide], 64, 1)
        o = out_rem[p].astype(F32)
        ret_part[2 * p, :, main:] = jnp.where(low, o, rem).astype(BF)
        ret_part[2 * p + 1, :, main:] = jnp.where(low, rem, o).astype(BF)

    for j in (1, 0):
        for h in (0, 1):
            comb(h, j)
    for j in (3, 2, 1):
        for h in (0, 1):
            fin(h, j)
    for h in (0, 1):
        init(h, 4)
    init2, comb2, fin2 = reduce(ret_part, ret_in, ret_in2, ret_res, 1)
    for j in (3, 2, 1, 0):
        for h in (0, 1):
            init2(h, j)
    for h in (0, 1):
        fin(h, 0)
        comb(h, 4)

    @pl.loop(0, n_pair)
    def _(p):
        gdown[:, span(p)] = dot(hid[...], grad_pair(p), ROWS).astype(BF)

    for h in (0, 1):
        fin(h, 4)
    scatter(out_res, lambda r: out_back.at[pl.ds(r, slot)], back_send.at[0], back_recv.at[0])
    for j in (3, 2):
        for h in (0, 1):
            comb2(h, j)

    @pl.loop(0, n_pair)
    def _(p):
        g = dot(tok_pair(p), gpre[...], ROWS).astype(BF)
        ggate[span(p)] = g[:, :128]
        gup[span(p)] = g[:, 128:]

    stores = [
        pltpu.make_async_copy(src, dst, gout_sem.at[i])
        for i, (src, dst) in enumerate(((ggate, ggate_hbm), (gup, gup_hbm), (gdown, gdown_hbm)))
    ]
    for store in stores:
        store.start()
    for j in (1, 0):
        for h in (0, 1):
            comb2(h, j)
    for j in (3, 2, 1):
        for h in (0, 1):
            fin2(h, j)
    for h in (0, 1):
        init2(h, 4)
    for h in (0, 1):
        comb2(h, 4)
    for h in (0, 1):
        fin2(h, 0)
    for h in (0, 1):
        fin2(h, 4)
    scatter(ret_res, lambda r: ret_back.at[pl.ds(r, slot)], back_send.at[1], back_recv.at[1])

    there = lax.broadcasted_iota(jnp.int32, (n_tok, rows), 0) == row_idx_ref[...]
    place = jnp.where(there, 1.0, 0.0).astype(BF)
    wait_bytes(out_back, back_recv.at[0])
    wait_bytes(ret_back, back_recv.at[1])
    unpack_a = packing(448 * odd, 384 + 64 * odd)
    unpack_b = packing(64 + 320 * odd, 448 - 64 * odd)
    out_rows = jnp.concatenate([out_back[...], ret_back[:, main:]], axis=1)
    scaled = dot(out_rows, unpack_a, LAST) * w_ref[...]
    high = scaled.astype(BF)
    rest = (scaled - high.astype(F32)).astype(BF)
    mixture_ref[...] = (dot(place, high) + dot(place, rest)).astype(BF)
    ret_rows = dot(ret_back[...], unpack_b, LAST).astype(BF)
    grad_tok_ref[...] = dot(place, ret_rows).astype(BF)

    wait_bytes(tok_loc.at[pl.ds(0, rows - slot)], a2a_send.at[0])
    wait_bytes(grad_loc.at[pl.ds(0, rows - slot)], a2a_send.at[1])
    wait_bytes(tok_all.at[pl.ds(0, 15)], ag_send.at[0])
    wait_bytes(grad_all.at[pl.ds(0, 15)], ag_send.at[1])
    wait_bytes(out_part.at[pl.ds(0, 15)], rs_send.at[0])
    wait_bytes(ret_part.at[pl.ds(0, 15)], rs_send.at[1])
    wait_bytes(out_res.at[pl.ds(0, rows - slot)], back_send.at[0])
    wait_bytes(ret_res.at[pl.ds(0, rows - slot)], back_send.at[1])
    for store in stores:
        store.wait()


def per_device(tokens, cotangent, gate_weight, up_weight, down_weight, chosen, counts, gate_prob):
    experts, _, slots = chosen.shape
    n_tok, feats = tokens.shape
    rows = experts * slots
    width = gate_weight.shape[1]
    hidden = gate_weight.shape[2]
    wide, main = 512, 384
    n = width // feats
    position = lax.broadcasted_iota(jnp.int32, (experts, slots), 1)
    live = position < counts
    index = jnp.where(live, chosen[:, 0, :], -1)
    weight = jnp.where(live, gate_prob[:, 0, :], 0.0)
    vmem = pl.BlockSpec(memory_space=pltpu.VMEM)
    hbm = pl.BlockSpec(memory_space=pl.ANY)
    dma = pltpu.SemaphoreType.DMA
    half = rows // 2
    outs = pl.pallas_call(
        kernel,
        out_shape=(
            jax.ShapeDtypeStruct((n_tok, feats), BF),
            jax.ShapeDtypeStruct((n_tok, feats), BF),
            jax.ShapeDtypeStruct((width, hidden), BF),
            jax.ShapeDtypeStruct((width, hidden), BF),
            jax.ShapeDtypeStruct((hidden, width), BF),
        ),
        in_specs=[vmem] * 5 + [hbm] * 3,
        out_specs=(vmem, vmem, hbm, hbm, hbm),
        scratch_shapes=[
            pltpu.VMEM((rows, wide), BF),
            pltpu.VMEM((rows, main), BF),
            pltpu.VMEM((n, rows, wide), BF),
            pltpu.VMEM((n, rows, main), BF),
            pltpu.VMEM((n // 2, rows, 128), BF),
            pltpu.VMEM((n // 2, rows, 128), BF),
            pltpu.VMEM((width, hidden), BF),
            pltpu.VMEM((width, hidden), BF),
            pltpu.VMEM((hidden, width), BF),
            pltpu.VMEM((width, hidden), BF),
            pltpu.VMEM((width, hidden), BF),
            pltpu.VMEM((hidden, width), BF),
            pltpu.VMEM((n, rows, main), BF),
            pltpu.VMEM((n // 2, rows, 128), BF),
            pltpu.VMEM((n, rows, wide), BF),
            pltpu.VMEM((rows, 2 * hidden), F32),
            pltpu.VMEM((rows, hidden), F32),
            pltpu.VMEM((rows, hidden), BF),
            pltpu.VMEM((rows, 2 * hidden), BF),
            pltpu.VMEM((2, 4, 3 * half, main), BF),
            pltpu.VMEM((2, 3 * half, main), BF),
            pltpu.VMEM((2, 4, 3 * half, wide), BF),
            pltpu.VMEM((2, 3 * half, wide), BF),
            pltpu.VMEM((rows, main), BF),
            pltpu.VMEM((rows, wide), BF),
            pltpu.VMEM((rows, main), BF),
            pltpu.VMEM((rows, wide), BF),
            dma((3,)),
            dma((2,)),
            dma((4,)),
            dma((2,)),
            dma((80,)),
            dma((2,)),
            dma((120,)),
            dma((2,)),
            dma((2,)),
            dma((3,)),
        ],
        compiler_params=pltpu.CompilerParams(
            collective_id=0, has_side_effects=True, vmem_limit_bytes=60 * 1024 * 1024
        ),
        name="experts",
    )(
        index.reshape(rows, 1),
        index.reshape(1, rows),
        weight.reshape(rows, 1),
        tokens,
        cotangent,
        gate_weight[0],
        up_weight[0],
        down_weight[0],
    )
    mixture, grad_tokens, grad_gate, grad_up, grad_down = outs
    return mixture, grad_tokens, grad_gate[None], grad_up[None], grad_down[None]


def solution(mesh):
    placed = (
        P("ep", "fsdp"),
        P("ep", "fsdp"),
        P("ep", None, "fsdp"),
        P("ep", None, "fsdp"),
        P("ep", "fsdp", None),
        P(None, "ep", None),
        P(None, "ep"),
        P(None, "ep", None),
    )
    return jax.shard_map(
        per_device,
        mesh=mesh,
        in_specs=placed,
        out_specs=(
            P("ep", "fsdp"),
            P("ep", "fsdp"),
            P("ep", None, "fsdp"),
            P("ep", None, "fsdp"),
            P("ep", "fsdp", None),
        ),
        check_vma=False,
    )
```

```python
import jax
import jax.numpy as jnp
from jax import lax
from jax.experimental import pallas as pl
from jax.experimental.pallas import tpu as pltpu
from jax.sharding import PartitionSpec as P

MESH = pl.DeviceIdType.MESH
BF = jnp.bfloat16
F32 = jnp.float32
SIDE = 4
RING = (0, -1, 1, 2)
LAST = (((1,), (1,)), ((), ()))
ROWS = (((0,), (0,)), ((), ()))


def dot(a, b, dims=(((1,), (0,)), ((), ()))):
    return lax.dot_general(a, b, dims, preferred_element_type=F32)


def packings(odd, feats, main, wide):
    fi = lax.broadcasted_iota(jnp.int32, (feats, wide), 0)
    fj = lax.broadcasted_iota(jnp.int32, (feats, wide), 1)

    def packing(delta, low):
        body = (fi == fj + 64 * odd) & (fj < main)
        tail = (fi == fj - delta) & (fj >= low) & (fj < low + 64)
        return jnp.where(body | tail, 1.0, 0.0).astype(BF)

    return packing(448 * odd, 384 + 64 * odd), packing(64 + 320 * odd, 448 - 64 * odd)


def kernel(
    count_ref, chosen_ref, prob_ref, tok_ref, cot_ref, gate_hbm, up_hbm, down_hbm,
    out_back, ret_back, hot_ref, w_ref, ggate, gup, gdown,
    tok_loc, grad_loc, tok_all, grad_all, tok_rem, grad_rem,
    gate, up, down,
    out_part, out_rem, ret_part, pre, gh, hid, gpre,
    out_in, out_in2, ret_in, ret_in2, out_res, ret_res,
    w_sem, a2a_send, a2a_recv, ag_send, ag_recv, rs_send, rs_recv, back_send, back_recv,
):
    f = lax.axis_index("fsdp")
    me = lax.axis_index("ep")
    n_ep = chosen_ref.shape[0]
    y = lax.div(f, SIDE)
    x = lax.rem(f, SIDE)
    odd = lax.rem(x, 2)
    wide = tok_all.shape[2]
    main = grad_all.shape[2]
    rows = tok_all.shape[1]
    half = rows // 2
    quarter = rows // 4
    feats = tok_ref.shape[0]
    pair = 2 * feats
    slot = 16

    def flat(dy, dx):
        return lax.rem(y + dy + SIDE, SIDE) * SIDE + lax.rem(x + dx + SIDE, SIDE)

    def coord(axis, along, other=0):
        return (other, along) if axis == 0 else (along, other)

    barrier = pltpu.get_barrier_semaphore()
    for dy, dx in ((0, 1), (0, -1), (1, 0), (-1, 0)):
        pl.semaphore_signal(barrier, inc=1, device_id={"fsdp": flat(dy, dx)}, device_id_type=MESH)

    @pl.loop(1, n_ep)
    def _(k):
        pl.semaphore_signal(barrier, inc=1, device_id={"ep": lax.rem(me + k, n_ep)}, device_id_type=MESH)

    loads = [
        pltpu.make_async_copy(src, dst, w_sem.at[i])
        for i, (src, dst) in enumerate(((gate_hbm, gate), (up_hbm, up), (down_hbm, down)))
    ]
    for load in loads:
        load.start()

    n_tok = tok_ref.shape[1]
    pack_a, pack_b = packings(odd, feats, main, wide)
    j = lax.broadcasted_iota(jnp.int32, (1, slot), 1)
    index, weight = [], []
    for e in range(n_ep):
        live = j < count_ref[e]
        index.append(jnp.broadcast_to(jnp.where(live, chosen_ref[e : e + 1], -1), (slot, slot)))
        weight.append(jnp.broadcast_to(jnp.where(live, prob_ref[e : e + 1], 0.0), (slot, slot)))
    shape = (rows, slot)
    mine = lax.rem(lax.broadcasted_iota(jnp.int32, shape, 0), slot) == lax.broadcasted_iota(jnp.int32, shape, 1)
    index = jnp.concatenate(index, axis=0).astype(F32)
    index = jnp.sum(jnp.where(mine, index, 0.0), axis=1, keepdims=True).astype(jnp.int32)
    weight = jnp.concatenate(weight, axis=0)
    w_ref[...] = jnp.sum(jnp.where(mine, weight, 0.0), axis=1, keepdims=True)
    hit = lax.broadcasted_iota(jnp.int32, (rows, n_tok), 1) == index
    onehot = jnp.where(hit, 1.0, 0.0).astype(BF)
    hot_ref[...] = onehot
    tp = dot(dot(onehot, tok_ref[...], LAST).astype(BF), pack_a)
    gp = dot((dot(onehot, cot_ref[...], LAST) * w_ref[...]).astype(BF), pack_b)
    tok_loc[:, :main] = tp[:, :main].astype(BF)
    tok_loc[:, main:] = (tp[:, main:] + gp[:, main:]).astype(BF)
    grad_loc[...] = gp[:, :main].astype(BF)

    pl.semaphore_wait(barrier, n_ep + 3)

    def scatter(src, dst_of, send, recv):
        @pl.loop(1, n_ep)
        def _(k):
            peer = lax.rem(me + k, n_ep)
            pltpu.make_async_remote_copy(
                src_ref=src.at[pl.ds(peer * slot, slot)],
                dst_ref=dst_of(me * slot),
                send_sem=send,
                recv_sem=recv,
                device_id={"ep": peer},
                device_id_type=MESH,
            ).start()

        pltpu.make_async_copy(src.at[pl.ds(me * slot, slot)], dst_of(me * slot), recv).start()

    def wait_bytes(ref, sem):
        pltpu.make_async_copy(ref, ref, sem).wait()

    part = lax.div(me, n_ep // 2)
    scatter(tok_loc, lambda r: tok_all.at[f, pl.ds(r, slot)], a2a_send.at[0], a2a_recv.at[part])
    scatter(grad_loc, lambda r: grad_all.at[f, pl.ds(r, slot)], a2a_send.at[1], a2a_recv.at[2 + part])

    def put(src, dst, send, recv, axis, step):
        dy, dx = coord(axis, step)
        pltpu.make_async_remote_copy(
            src_ref=src, dst_ref=dst, send_sem=send, recv_sem=recv,
            device_id={"fsdp": flat(dy, dx)}, device_id_type=MESH,
        ).start()

    def gather(buf, which):
        send = ag_send.at[which]

        def sem(h, i):
            return ag_recv.at[which * 40 + h * 20 + i]

        def ref(h, fst, snd, q=None):
            o = coord(h, fst, snd)
            first = h * half + (0 if q is None else q * quarter)
            return buf.at[flat(*o), pl.ds(first, half if q is None else quarter)]

        def wait(h, i, fst, snd, q=None):
            wait_bytes(ref(h, fst, snd, q), sem(h, i))

        def send_block(h, i, fst, snd, axis, step, q=None):
            r = ref(h, fst, snd, q)
            put(r, r, send, sem(h, i), axis, step)

        def own(h):
            for i, step in ((0, 1), (1, -1)):
                send_block(h, i, 0, 0, h, step)
            for i, step in ((4, 1), (5, -1)):
                send_block(h, i, 0, 0, 1 - h, step)

        def spread(h, j):
            for i, step in ((0, 1), (1, -1)):
                send_block(h, 4 + 4 * j + i, RING[j], 0, 1 - h, step)

        def s1():
            for i in (0, 1):
                o = (-1, 1)[i]
                for h in (0, 1):
                    wait(h, i, o, 0)
                    send_block(h, 2 + i, o, 0, h, -o, i)
                for h in (0, 1):
                    spread(h, 1 + i)

        def relay(j):
            for i in (0, 1):
                o = (-1, 1)[i]
                for h in (1, 0):
                    wait(h, 4 + 4 * j + i, RING[j], o)
                    send_block(h, 6 + 4 * j + i, RING[j], o, 1 - h, -o, i)

        def s3():
            for h in (0, 1):
                wait(h, 2, 2, 0, 0)
                wait(h, 3, 2, 0, 1)
                spread(h, 3)

        def finish():
            for j in range(4):
                for h in (0, 1):
                    for i in (0, 1):
                        wait(h, 6 + 4 * j + i, RING[j], 2, i)

        return own, s1, relay, s3, finish

    def reduce(buf, in1, in2, res, which):
        send = rs_send.at[which]
        order = (3, 2, 1, 0)

        def sem(h, j, i):
            return rs_recv.at[which * 60 + h * 30 + j * 6 + i]

        def piece(h, fst, snd, q=None):
            o = coord(h, fst, snd)
            first = h * half + (0 if q is None else q * quarter)
            return buf.at[flat(*o), pl.ds(first, half if q is None else quarter)]

        def land(h, j, first, n):
            if j < 4:
                return in1.at[h, j, pl.ds(first, n)]
            return in2.at[h, pl.ds(first, n)]

        def term(h, j, k, q=None):
            if j < 4:
                return piece(h, RING[j], k, q)
            return piece(h, k, 0, q)

        q1, q2, fp, fm = 0, quarter, half, 2 * half

        def axis_of(h, j):
            return 1 - h if j < 4 else h

        def init(h, j):
            ax = axis_of(h, j)
            put(term(h, j, 2, 0), land(h, j, q1, quarter), send, sem(h, j, 0), ax, 1)
            put(term(h, j, 2, 1), land(h, j, q2, quarter), send, sem(h, j, 1), ax, -1)
            put(term(h, j, 1, 1), land(h, j, fp + quarter, quarter), send, sem(h, j, 2), ax, 1)
            put(term(h, j, -1, 0), land(h, j, fm, quarter), send, sem(h, j, 3), ax, -1)

        def comb(h, j):
            ax = axis_of(h, j)
            for i, k, first, dst in ((0, 1, q1, fp), (1, -1, q2, fm + quarter)):
                r = land(h, j, first, quarter)
                wait_bytes(r, sem(h, j, i))
                r[...] = (r[...].astype(F32) + term(h, j, k, i)[...].astype(F32)).astype(BF)
                put(r, land(h, j, dst, quarter), send, sem(h, j, 4 + i), ax, k)

        def fin(h, j):
            for first, i in ((fp + quarter, 2), (fm, 3), (fp, 4), (fm + quarter, 5)):
                wait_bytes(land(h, j, first, quarter), sem(h, j, i))
            own = term(h, j, 0)
            total = (
                own[...].astype(F32)
                + land(h, j, fp, half)[...].astype(F32)
                + land(h, j, fm, half)[...].astype(F32)
            ).astype(BF)
            if j < 4:
                own[...] = total
            else:
                res[pl.ds(h * half, half)] = total

        return init, comb, fin

    own, s1, relay, s3, finish = gather(tok_all, 0)
    for h in (0, 1):
        wait_bytes(tok_all.at[f, pl.ds(h * half, half)], a2a_recv.at[h])
        own(h)
    s1()
    relay(0)
    s3()
    relay(1)
    relay(2)
    relay(3)
    own2, s1b, relay2, s3b, finish2 = gather(grad_all, 1)
    for h in (0, 1):
        wait_bytes(grad_all.at[f, pl.ds(h * half, half)], a2a_recv.at[2 + h])
        own2(h)
    finish()

    n_pair = tok_all.shape[0] // 2
    low = lax.broadcasted_iota(jnp.int32, (rows, 128), 1) < 64
    for load in loads:
        load.wait()

    def span(p, size=pair):
        return pl.ds(pl.multiple_of(p * pair, 128), size)

    def tok_pair(p):
        return jnp.concatenate(
            [tok_all[2 * p, :, :main], tok_rem[p], tok_all[2 * p + 1, :, :main]], axis=1
        )

    def grad_pair(p):
        return jnp.concatenate([grad_all[2 * p], grad_rem[p], grad_all[2 * p + 1]], axis=1)

    pre[...] = jnp.zeros_like(pre)
    gh[...] = jnp.zeros_like(gh)

    @pl.loop(0, n_pair)
    def _(p):
        even = tok_all[2 * p, :, main:].astype(F32)
        other = tok_all[2 * p + 1, :, main:].astype(F32)
        tok_rem[p] = jnp.where(low, even, other).astype(BF)
        grad_rem[p] = pltpu.roll(jnp.where(low, other, even), 64, 1).astype(BF)
        both = jnp.concatenate([gate[span(p)], up[span(p)]], axis=1)
        pre[...] += dot(tok_pair(p), both)

    pg = pre[:, :128]
    pu = pre[:, 128:]
    sg = jax.nn.sigmoid(pg)
    hid[...] = (pg * sg * pu).astype(BF)
    s1b()
    relay2(0)

    @pl.loop(0, n_pair)
    def _(p):
        o = dot(hid[...], down[:, span(p)]).astype(BF)
        out_part[2 * p] = o[:, :main]
        out_rem[p] = o[:, main:wide]
        out_part[2 * p + 1] = o[:, wide:]

    s3b()
    relay2(1)
    relay2(2)
    relay2(3)
    init, comb, fin = reduce(out_part, out_in, out_in2, out_res, 0)
    for j in (3, 2, 1, 0):
        for h in (0, 1):
            init(h, j)
    finish2()

    @pl.loop(0, n_pair)
    def _(p):
        gh[...] += dot(grad_pair(p), down[:, span(p)], LAST)

    pg = pre[:, :128]
    pu = pre[:, 128:]
    sg = jax.nn.sigmoid(pg)
    gpre[:, :128] = (gh[...] * pu * sg * (1.0 + pg * (1.0 - sg))).astype(BF)
    gpre[:, 128:] = (gh[...] * (pg * sg)).astype(BF)
    for j in (3, 2):
        for h in (0, 1):
            comb(h, j)

    @pl.loop(0, n_pair)
    def _(p):
        both = jnp.concatenate([gate[span(p)], up[span(p)]], axis=1)
        r = dot(gpre[...], both, LAST)
        ret_part[2 * p, :, :main] = r[:, :main].astype(BF)
        ret_part[2 * p + 1, :, :main] = r[:, wide:].astype(BF)
        rem = pltpu.roll(r[:, main:wide], 64, 1)
        o = out_rem[p].astype(F32)
        ret_part[2 * p, :, main:] = jnp.where(low, o, rem).astype(BF)
        ret_part[2 * p + 1, :, main:] = jnp.where(low, rem, o).astype(BF)

    for j in (1, 0):
        for h in (0, 1):
            comb(h, j)
    for j in (3, 2, 1):
        for h in (0, 1):
            fin(h, j)
    for h in (0, 1):
        init(h, 4)
    init2, comb2, fin2 = reduce(ret_part, ret_in, ret_in2, ret_res, 1)
    for j in (3, 2, 1, 0):
        for h in (0, 1):
            init2(h, j)
    for h in (0, 1):
        fin(h, 0)
        comb(h, 4)

    @pl.loop(0, n_pair)
    def _(p):
        gdown[:, span(p)] = dot(hid[...], grad_pair(p), ROWS).astype(BF)

    for h in (0, 1):
        fin(h, 4)
    scatter(out_res, lambda r: out_back.at[pl.ds(r, slot)], back_send.at[0], back_recv.at[0])
    for j in (3, 2):
        for h in (0, 1):
            comb2(h, j)

    @pl.loop(0, n_pair)
    def _(p):
        g = dot(tok_pair(p), gpre[...], ROWS).astype(BF)
        ggate[span(p)] = g[:, :128]
        gup[span(p)] = g[:, 128:]

    for j in (1, 0):
        for h in (0, 1):
            comb2(h, j)
    for j in (3, 2, 1):
        for h in (0, 1):
            fin2(h, j)
    for h in (0, 1):
        init2(h, 4)
    for h in (0, 1):
        comb2(h, 4)
    for h in (0, 1):
        fin2(h, 0)
    for h in (0, 1):
        fin2(h, 4)
    scatter(ret_res, lambda r: ret_back.at[pl.ds(r, slot)], back_send.at[1], back_recv.at[1])

    wait_bytes(out_back, back_recv.at[0])
    wait_bytes(ret_back, back_recv.at[1])

    wait_bytes(tok_loc.at[pl.ds(0, rows - slot)], a2a_send.at[0])
    wait_bytes(grad_loc.at[pl.ds(0, rows - slot)], a2a_send.at[1])
    wait_bytes(tok_all.at[pl.ds(0, 15)], ag_send.at[0])
    wait_bytes(grad_all.at[pl.ds(0, 15)], ag_send.at[1])
    wait_bytes(out_part.at[pl.ds(0, 15)], rs_send.at[0])
    wait_bytes(ret_part.at[pl.ds(0, 15)], rs_send.at[1])
    wait_bytes(out_res.at[pl.ds(0, rows - slot)], back_send.at[0])
    wait_bytes(ret_res.at[pl.ds(0, rows - slot)], back_send.at[1])


def finish_kernel(
    out_ref, ret_ref, hot_ref, w_ref, ggate, gup, gdown,
    mixture_ref, grad_tok_ref, ggate_hbm, gup_hbm, gdown_hbm, sem,
):
    stores = [
        pltpu.make_async_copy(src, dst, sem.at[i])
        for i, (src, dst) in enumerate(((ggate, ggate_hbm), (gup, gup_hbm), (gdown, gdown_hbm)))
    ]
    for store in stores:
        store.start()
    odd = lax.rem(lax.axis_index("fsdp"), 2)
    feats = mixture_ref.shape[0]
    main, wide = out_ref.shape[1], ret_ref.shape[1]
    unpack_a, unpack_b = packings(odd, feats, main, wide)
    out_rows = jnp.concatenate([out_ref[...], ret_ref[:, main:]], axis=1)
    scaled = out_rows.astype(F32) * w_ref[...]
    high = scaled.astype(BF)
    rest = (scaled - high.astype(F32)).astype(BF)
    hot = hot_ref[...]
    high = dot(unpack_a, high, LAST).astype(BF)
    rest = dot(unpack_a, rest, LAST).astype(BF)
    mixture_ref[...] = (dot(high, hot) + dot(rest, hot)).astype(BF)
    grad_tok_ref[...] = dot(dot(unpack_b, ret_ref[...], LAST).astype(BF), hot).astype(BF)
    for store in stores:
        store.wait()


def per_device(tokens, cotangent, gate_weight, up_weight, down_weight, chosen, counts, gate_prob):
    experts, _, slots = chosen.shape
    n_tok, feats = tokens.shape
    rows = experts * slots
    width = gate_weight.shape[1]
    hidden = gate_weight.shape[2]
    wide, main = 512, 384
    n = width // feats
    vmem = pl.BlockSpec(memory_space=pltpu.VMEM)
    smem = pl.BlockSpec(memory_space=pltpu.SMEM)
    hbm = pl.BlockSpec(memory_space=pl.ANY)
    dma = pltpu.SemaphoreType.DMA
    half = rows // 2
    kept = pl.pallas_call(
        kernel,
        out_shape=(
            pltpu.VMEM((rows, main), BF),
            pltpu.VMEM((rows, wide), BF),
            pltpu.VMEM((rows, n_tok), BF),
            pltpu.VMEM((rows, 1), F32),
            pltpu.VMEM((width, hidden), BF),
            pltpu.VMEM((width, hidden), BF),
            pltpu.VMEM((hidden, width), BF),
        ),
        in_specs=[smem] + [vmem] * 4 + [hbm] * 3,
        out_specs=(vmem,) * 7,
        scratch_shapes=[
            pltpu.VMEM((rows, wide), BF),
            pltpu.VMEM((rows, main), BF),
            pltpu.VMEM((n, rows, wide), BF),
            pltpu.VMEM((n, rows, main), BF),
            pltpu.VMEM((n // 2, rows, 128), BF),
            pltpu.VMEM((n // 2, rows, 128), BF),
            pltpu.VMEM((width, hidden), BF),
            pltpu.VMEM((width, hidden), BF),
            pltpu.VMEM((hidden, width), BF),
            pltpu.VMEM((n, rows, main), BF),
            pltpu.VMEM((n // 2, rows, 128), BF),
            pltpu.VMEM((n, rows, wide), BF),
            pltpu.VMEM((rows, 2 * hidden), F32),
            pltpu.VMEM((rows, hidden), F32),
            pltpu.VMEM((rows, hidden), BF),
            pltpu.VMEM((rows, 2 * hidden), BF),
            pltpu.VMEM((2, 4, 3 * half, main), BF),
            pltpu.VMEM((2, 3 * half, main), BF),
            pltpu.VMEM((2, 4, 3 * half, wide), BF),
            pltpu.VMEM((2, 3 * half, wide), BF),
            pltpu.VMEM((rows, main), BF),
            pltpu.VMEM((rows, wide), BF),
            dma((3,)),
            dma((2,)),
            dma((4,)),
            dma((2,)),
            dma((80,)),
            dma((2,)),
            dma((120,)),
            dma((2,)),
            dma((2,)),
        ],
        compiler_params=pltpu.CompilerParams(
            collective_id=0, has_side_effects=True, vmem_limit_bytes=52 * 1024 * 1024
        ),
        name="experts",
    )(
        counts[:, 0],
        chosen[:, 0, :],
        gate_prob[:, 0, :],
        tokens.T,
        cotangent.T,
        gate_weight[0],
        up_weight[0],
        down_weight[0],
    )
    mixture, grad_tokens, grad_gate, grad_up, grad_down = pl.pallas_call(
        finish_kernel,
        out_shape=(
            jax.ShapeDtypeStruct((feats, n_tok), BF),
            jax.ShapeDtypeStruct((feats, n_tok), BF),
            jax.ShapeDtypeStruct((width, hidden), BF),
            jax.ShapeDtypeStruct((width, hidden), BF),
            jax.ShapeDtypeStruct((hidden, width), BF),
        ),
        in_specs=[vmem] * 7,
        out_specs=(vmem, vmem, hbm, hbm, hbm),
        scratch_shapes=[dma((3,))],
        compiler_params=pltpu.CompilerParams(vmem_limit_bytes=16 * 1024 * 1024),
        name="finish",
    )(*kept)
    return mixture.T, grad_tokens.T, grad_gate[None], grad_up[None], grad_down[None]


def solution(mesh):
    placed = (
        P("ep", "fsdp"),
        P("ep", "fsdp"),
        P("ep", None, "fsdp"),
        P("ep", None, "fsdp"),
        P("ep", "fsdp", None),
        P(None, "ep", None),
        P(None, "ep"),
        P(None, "ep", None),
    )
    return jax.shard_map(
        per_device,
        mesh=mesh,
        in_specs=placed,
        out_specs=(
            P("ep", "fsdp"),
            P("ep", "fsdp"),
            P("ep", None, "fsdp"),
            P("ep", None, "fsdp"),
            P("ep", "fsdp", None),
        ),
        check_vma=False,
    )
```

```python
import jax
import jax.numpy as jnp
from jax import lax
from jax.experimental import pallas as pl
from jax.experimental.pallas import tpu as pltpu
from jax.sharding import PartitionSpec as P

MESH = pl.DeviceIdType.MESH
BF = jnp.bfloat16
F32 = jnp.float32
SIDE = 4
RING = (0, -1, 1, 2)
LAST = (((1,), (1,)), ((), ()))
ROWS = (((0,), (0,)), ((), ()))


def dot(a, b, dims=(((1,), (0,)), ((), ()))):
    return lax.dot_general(a, b, dims, preferred_element_type=F32)


def packings(odd, feats, main, wide):
    fi = lax.broadcasted_iota(jnp.int32, (feats, main), 0)
    fj = lax.broadcasted_iota(jnp.int32, (feats, main), 1)
    body = jnp.where(fi - fj == 64 * odd, 1.0, 0.0)
    ti = lax.broadcasted_iota(jnp.int32, (feats, wide - main), 0)
    tj = lax.broadcasted_iota(jnp.int32, (feats, wide - main), 1)
    where = jnp.where(odd == 1, ti, ti - main)

    def packing(low):
        tail = jnp.where((tj - where == low) & (tj >= low) & (tj < low + 64), 1.0, 0.0)
        return jnp.concatenate([body, tail], axis=1).astype(BF)

    return packing(64 * odd), packing(64 - 64 * odd)


def kernel(
    count_ref, chosen_ref, prob_ref, tok_ref, cot_ref, gate_hbm, up_hbm, down_hbm,
    mixture_ref, grad_tok_ref, ggate, gup, gdown,
    out_back, ret_back, hot_ref, w_ref, pack_ref,
    tok_loc, grad_loc, tok_all, grad_all, tok_rem, grad_rem,
    gate, up, down, down_ring, down_relay, gd_part, gd_relay,
    hid, hid_t, hid_g, gh_send, gh_own, gh_in, pre, gpre,
    out_part, ret_part, out_in, ret_in, ret_in2, out_res, ret_res,
    w_sem, a2a_send, a2a_recv, ag_send, ag_recv, rs_send, rs_recv, out_recv, back_send, back_recv,
    swap_send, swap_recv, small_send, small_recv,
):
    f = lax.axis_index("fsdp")
    me = lax.axis_index("ep")
    n_ep = chosen_ref.shape[0]
    y = lax.div(f, SIDE)
    x = lax.rem(f, SIDE)
    odd = lax.rem(x, 2)
    wide = tok_all.shape[2]
    main = grad_all.shape[2]
    rows = tok_all.shape[1]
    half = rows // 2
    quarter = rows // 4
    feats = tok_ref.shape[0]
    pair = 2 * feats
    slot = 16
    unit = 64

    def flat(dy, dx):
        return lax.rem(y + dy + SIDE, SIDE) * SIDE + lax.rem(x + dx + SIDE, SIDE)

    def coord(axis, along, other=0):
        return (other, along) if axis == 0 else (along, other)

    def place(o):
        return RING.index(o)

    barrier = pltpu.get_barrier_semaphore()
    for axis in (0, 1):
        for o in (1, -1, 2):
            pl.semaphore_signal(barrier, inc=1, device_id={"fsdp": flat(*coord(axis, o))}, device_id_type=MESH)

    @pl.loop(1, n_ep)
    def _(k):
        pl.semaphore_signal(barrier, inc=1, device_id={"ep": lax.rem(me + k, n_ep)}, device_id_type=MESH)

    loads = [
        pltpu.make_async_copy(src, dst, w_sem.at[i])
        for i, (src, dst) in enumerate(((down_hbm, down), (gate_hbm, gate), (up_hbm, up)))
    ]
    for load in loads:
        load.start()

    def wait_bytes(ref, sem):
        pltpu.make_async_copy(ref, ref, sem).wait()

    def put(src, dst, send, recv, axis, step):
        pltpu.make_async_remote_copy(
            src_ref=src, dst_ref=dst, send_sem=send, recv_sem=recv,
            device_id={"fsdp": flat(*coord(axis, step))}, device_id_type=MESH,
        ).start()

    def lanes(h, along, other):
        slice_ = flat(*coord(h, along, other))
        first = pair * lax.div(slice_, 2) + wide * lax.rem(slice_, 2)
        return pl.ds(pl.multiple_of(first, 128), main)

    def owned(ref, h, along, other):
        return ref.at[pl.ds(h * unit, unit), lanes(h, along, other)]

    def block(i):
        return pl.ds(i * unit, unit)

    n_tok = tok_ref.shape[1]
    pack_a, pack_b = packings(odd, feats, main, wide)
    pack_ref[0] = pack_a
    pack_ref[1] = pack_b
    j = lax.broadcasted_iota(jnp.int32, (1, slot), 1)
    index, weight = [], []
    for e in range(n_ep):
        live = j < count_ref[e]
        index.append(jnp.broadcast_to(jnp.where(live, chosen_ref[e : e + 1], -1), (slot, slot)))
        weight.append(jnp.broadcast_to(jnp.where(live, prob_ref[e : e + 1], 0.0), (slot, slot)))
    shape = (rows, slot)
    mine = lax.rem(lax.broadcasted_iota(jnp.int32, shape, 0), slot) == lax.broadcasted_iota(jnp.int32, shape, 1)
    index = jnp.concatenate(index, axis=0).astype(F32)
    index = jnp.sum(jnp.where(mine, index, 0.0), axis=1, keepdims=True).astype(jnp.int32)
    weight = jnp.concatenate(weight, axis=0)
    w_ref[...] = jnp.sum(jnp.where(mine, weight, 0.0), axis=1, keepdims=True)
    hit = lax.broadcasted_iota(jnp.int32, (rows, n_tok), 1) == index
    onehot = jnp.where(hit, 1.0, 0.0).astype(BF)
    hot_ref[...] = onehot

    loads[0].wait()
    pl.semaphore_wait(barrier, n_ep + 5)

    for i in (0, 1):
        for h in (0, 1):
            for d, step in ((0, 1), (1, -1)):
                put(owned(down, h, 2, RING[2 * d + i]), down_relay.at[h, d, i],
                    swap_send.at[0], swap_recv.at[2 * h + d], h, step)
    for c in range(4):
        for h in (0, 1):
            for step in (1, -1):
                put(owned(down, h, step, RING[c]), down_ring.at[h, c, block(place(-step))],
                    swap_send.at[0], swap_recv.at[4 + h], h, step)


    tp = dot(dot(onehot, tok_ref[...], LAST).astype(BF), pack_a)
    gp = dot((dot(onehot, cot_ref[...], LAST) * w_ref[...]).astype(BF), pack_b)
    tok_loc[:, :main] = tp[:, :main].astype(BF)
    tok_loc[:, main:] = (tp[:, main:] + gp[:, main:]).astype(BF)
    grad_loc[...] = gp[:, :main].astype(BF)

    def scatter(src, dst_of, send, recv):
        @pl.loop(1, n_ep)
        def _(k):
            peer = lax.rem(me + k, n_ep)
            pltpu.make_async_remote_copy(
                src_ref=src.at[pl.ds(peer * slot, slot)],
                dst_ref=dst_of(me * slot),
                send_sem=send,
                recv_sem=recv,
                device_id={"ep": peer},
                device_id_type=MESH,
            ).start()

        pltpu.make_async_copy(src.at[pl.ds(me * slot, slot)], dst_of(me * slot), recv).start()

    part = lax.div(me, n_ep // 2)
    scatter(grad_loc, lambda r: grad_all.at[f, pl.ds(r, slot)], a2a_send.at[1], a2a_recv.at[2])
    scatter(tok_loc, lambda r: tok_all.at[f, pl.ds(r, slot)], a2a_send.at[0], a2a_recv.at[part])

    def swap_relay():
        for h in (0, 1):
            for d, step in ((0, 1), (1, -1)):
                wait_bytes(down_relay.at[h, d], swap_recv.at[2 * h + d])
                for i in (0, 1):
                    put(down_relay.at[h, d, i], down_ring.at[h, 2 * d + i, block(place(2))],
                        swap_send.at[0], swap_recv.at[4 + h], h, step)

    for h in (0, 1):
        for c in range(4):
            down_ring[h, c, :unit] = down[h * unit : (h + 1) * unit, lanes(h, 0, RING[c])]
    swap_relay()

    def gather(buf, send):
        def sem(h, i):
            return ag_recv.at[h * 20 + i]

        def ref(h, fst, snd, q=None):
            o = coord(h, fst, snd)
            first = h * half + (0 if q is None else q * quarter)
            return buf.at[flat(*o), pl.ds(first, half if q is None else quarter)]

        def wait(h, i, fst, snd, q=None):
            wait_bytes(ref(h, fst, snd, q), sem(h, i))

        def send_block(h, i, fst, snd, axis, step, q=None):
            r = ref(h, fst, snd, q)
            put(r, r, send, sem(h, i), axis, step)

        def own(h):
            for i, step in ((0, 1), (1, -1)):
                send_block(h, i, 0, 0, h, step)
            for i, step in ((4, 1), (5, -1)):
                send_block(h, i, 0, 0, 1 - h, step)

        def spread(h, j):
            for i, step in ((0, 1), (1, -1)):
                send_block(h, 4 + 4 * j + i, RING[j], 0, 1 - h, step)

        def s1():
            for i in (0, 1):
                o = (-1, 1)[i]
                for h in (0, 1):
                    wait(h, i, o, 0)
                    send_block(h, 2 + i, o, 0, h, -o, i)
                for h in (0, 1):
                    spread(h, 1 + i)

        def relay(j):
            for i in (0, 1):
                o = (-1, 1)[i]
                for h in (1, 0):
                    wait(h, 4 + 4 * j + i, RING[j], o)
                    send_block(h, 6 + 4 * j + i, RING[j], o, 1 - h, -o, i)

        def s3():
            for h in (0, 1):
                wait(h, 2, 2, 0, 0)
                wait(h, 3, 2, 0, 1)
                spread(h, 3)

        def finish():
            for j in range(4):
                for h in (0, 1):
                    for i in (0, 1):
                        wait(h, 6 + 4 * j + i, RING[j], 2, i)

        return own, s1, relay, s3, finish

    def ring(axis, term, land, n, sem, send):
        q1, q2, fp, fm = 0, n, 2 * n, 4 * n

        def init():
            put(term(2, 0), land(q1, n), send, sem(0), axis, 1)
            put(term(2, 1), land(q2, n), send, sem(1), axis, -1)
            put(term(1, 1), land(fp + n, n), send, sem(2), axis, 1)
            put(term(-1, 0), land(fm, n), send, sem(3), axis, -1)

        def comb():
            for i, k, first, dst in ((0, 1, q1, fp), (1, -1, q2, fm + n)):
                r = land(first, n)
                wait_bytes(r, sem(i))
                r[...] = (r[...].astype(F32) + term(k, i)[...].astype(F32)).astype(BF)
                put(r, land(dst, n), send, sem(4 + i), axis, k)

        def total():
            for first, i in ((fp + n, 2), (fm, 3), (fp, 4), (fm + n, 5)):
                wait_bytes(land(first, n), sem(i))
            return (
                term(0)[...].astype(F32)
                + land(fp, 2 * n)[...].astype(F32)
                + land(fm, 2 * n)[...].astype(F32)
            )

        return init, comb, total

    def reduce(buf, in1, in2, res, send):
        def make(h, j):
            def term(k, q=None):
                o = coord(h, RING[j], k) if j < 4 else coord(h, k, 0)
                first = h * half + (0 if q is None else q * quarter)
                return buf.at[flat(*o), pl.ds(first, half if q is None else quarter)]

            def land(first, n):
                if j < 4:
                    return in1.at[h, j, pl.ds(first, n)]
                return in2.at[h, pl.ds(first, n)]

            def sem(i):
                return rs_recv.at[h * 30 + j * 6 + i]

            init, comb, total = ring(1 - h if j < 4 else h, term, land, quarter, sem, send)

            def fin():
                if j < 4:
                    term(0)[...] = total().astype(BF)
                else:
                    res[pl.ds(h * half, half)] = total().astype(BF)

            return init, comb, fin

        return {(h, j): make(h, j) for h in (0, 1) for j in range(5)}

    def grad_block(axis, o, q=None):
        g = grad_all.at[flat(*coord(axis, o))]
        return g if q is None else g.at[pl.ds(q * half, half)]

    def grad_sem(axis, i):
        return ag_recv.at[40 + axis * 4 + i]

    wait_bytes(grad_all.at[f], a2a_recv.at[2])
    for axis in (0, 1):
        for i, step in ((0, 1), (1, -1)):
            put(grad_block(axis, 0), grad_block(axis, 0), ag_send.at[1], grad_sem(axis, i), axis, step)
    own, s1, relay, s3, finish = gather(tok_all, ag_send.at[0])
    for h in (0, 1):
        wait_bytes(tok_all.at[f, pl.ds(h * half, half)], a2a_recv.at[h])
        own(h)
    for i in (0, 1):
        o = (-1, 1)[i]
        for axis in (0, 1):
            wait_bytes(grad_block(axis, o), grad_sem(axis, i))
            put(grad_block(axis, o, i), grad_block(axis, o, i), ag_send.at[1], grad_sem(axis, 2 + i), axis, -o)
    s1()

    def grad_hidden(h):
        wait_bytes(down_ring.at[h, pl.ds(0, 3)], swap_recv.at[4 + h])
        for i in (0, 1):
            wait_bytes(grad_block(1 - h, 2, i), grad_sem(1 - h, 2 + i))
        term = jnp.zeros((4 * unit, rows), F32)
        for c in range(4):
            term = term + dot(down_ring[h, c], grad_block(1 - h, RING[c])[...], LAST)
        gh_own[pl.ds(h * unit, unit)] = term[:unit]
        gh_send[h] = term[unit:].astype(BF)
        for o in (2, 1, -1):
            put(gh_send.at[h, block(place(o) - 1)], gh_in.at[h, place(-o if o < 2 else 2) - 1],
                small_send.at[2 + h], small_recv.at[2 + h], h, o)

    grad_hidden(0)
    relay(0)
    grad_hidden(1)
    s3()
    relay(1)
    relay(2)
    relay(3)
    n_pair = tok_all.shape[0] // 2
    low = lax.broadcasted_iota(jnp.int32, (half, 128), 1) < 64

    def span(p, size=pair):
        return pl.ds(pl.multiple_of(p * pair, 128), size)

    def rest(p):
        return pl.ds(pl.multiple_of(p * pair + main, 128), 128)

    def tok_pair(p, r=slice(None)):
        return jnp.concatenate(
            [tok_all[2 * p, r, :main], tok_rem[p, r], tok_all[2 * p + 1, r, :main]], axis=1
        )

    def row_at(d):
        return lax.rem(y + d, SIDE)

    def accumulate(p, h):
        r = pl.ds(h * half, half)
        even = tok_all[2 * p, r, main:].astype(F32)
        other = tok_all[2 * p + 1, r, main:].astype(F32)
        tok_rem[p, r] = jnp.where(low, even, other).astype(BF)
        grad_rem[p, r] = pltpu.roll(jnp.where(low, other, even), 64, 1).astype(BF)
        both = jnp.concatenate([gate[span(p)], up[span(p)]], axis=1)
        pre[r] += dot(tok_pair(p, r), both)
        gh_own[:, r] += dot(down[:, rest(p)], grad_rem[p, r], LAST)

    pre[...] = jnp.zeros_like(pre)
    loads[1].wait()
    loads[2].wait()

    @pl.loop(0, 6)
    def _(t):
        accumulate(2 * row_at(3 + lax.div(t, 2)) + lax.rem(t, 2), 0)

    @pl.loop(0, 4)
    def _(t):
        accumulate(2 * t + lax.div(x, 2), 1)

    for h in (0, 1):
        wait_bytes(gh_in.at[h], small_recv.at[2 + h])
        gh_own[pl.ds(h * unit, unit)] += (
            gh_in[h, 0].astype(F32) + gh_in[h, 1].astype(F32) + gh_in[h, 2].astype(F32)
        )
    finish()
    xp = lax.div(x, 2)
    for h in (0, 1):
        @pl.loop(0, (2, 4)[h])
        def _(t, h=h):
            accumulate((2 * row_at(2) + t, 2 * t + 1 - xp)[h], h)

    pg = pre[:, :128]
    pu = pre[:, 128:]
    sg = jax.nn.sigmoid(pg)
    hidden = pg * sg * pu
    hid[...] = hidden.astype(BF)
    turned = jnp.transpose(hidden).astype(BF)
    for h in (0, 1):
        hid_t[h, :unit] = turned[h * unit : (h + 1) * unit]
    for o in (2, 1, -1):
        for h in (0, 1):
            put(hid_t.at[h, block(0)], hid_t.at[h, block(place(-o if o < 2 else 2))],
                small_send.at[h], small_recv.at[h], h, o)
    gh = jnp.transpose(gh_own[...])
    gpre[:, :128] = (gh * pu * sg * (1.0 + pg * (1.0 - sg))).astype(BF)
    gpre[:, 128:] = (gh * (pg * sg)).astype(BF)
    wlow = lax.broadcasted_iota(jnp.int32, (rows, 128), 1) < 64

    def ret_pair(p):
        both = jnp.concatenate([gate[span(p)], up[span(p)]], axis=1)
        r = dot(gpre[...], both, LAST)
        ret_part[2 * p, :, :main] = r[:, :main].astype(BF)
        ret_part[2 * p + 1, :, :main] = r[:, wide:].astype(BF)
        rem = pltpu.roll(r[:, main:wide], 64, 1)
        o = dot(hid[...], down[:, rest(p)])
        ret_part[2 * p, :, main:] = jnp.where(wlow, o, rem).astype(BF)
        ret_part[2 * p + 1, :, main:] = jnp.where(wlow, rem, o).astype(BF)

    rets = reduce(ret_part, ret_in, ret_in2, ret_res, rs_send.at[1])

    def each(step, *order):
        for j in order:
            for h in (0, 1):
                rets[h, j][step]()

    @pl.loop(0, 2)
    def _(t):
        ret_pair(2 * row_at(2) + t)

    rets[1, 3][0]()

    @pl.loop(3, 6)
    def _(t):
        ret_pair(2 * row_at(t) + 1 - xp)

    rets[0, 3][0]()

    @pl.loop(3, 6)
    def _(t):
        ret_pair(2 * row_at(t) + xp)

    each(0, 2, 1, 0)

    outs = []
    for h in (0, 1):
        wait_bytes(hid_t.at[h, pl.ds(0, 3 * unit)], small_recv.at[h])
        hid_g[h] = jnp.transpose(hid_t[h].astype(F32)).astype(BF)
        for c in range(4):
            out_part[h, c] = dot(hid_g[h], down_ring[h, c]).astype(BF)

        def term(k, q=None, h=h):
            r = out_part.at[h, place(k)]
            return r if q is None else r.at[pl.ds(q * half, half)]

        def land(first, n, h=h):
            return out_in.at[h, pl.ds(first, n)]

        outs.append(ring(1 - h, term, land, half, lambda i, h=h: out_recv.at[h * 6 + i], rs_send.at[0]))
        outs[h][0]()
    each(1, 3, 2)

    @pl.loop(0, n_pair)
    def _(p):
        g = dot(tok_pair(p), gpre[...], ROWS).astype(BF)
        ggate[span(p)] = g[:, :128]
        gup[span(p)] = g[:, 128:]
        gdown[:, rest(p)] = dot(hid[...], grad_rem[p], ROWS).astype(BF)

    each(1, 1, 0)
    for h in (0, 1):
        for c in range(4):
            gd_part[h, c] = dot(hid_t[h], grad_block(1 - h, RING[c])[...]).astype(BF)
            gdown[h * unit : (h + 1) * unit, lanes(h, 0, RING[c])] = gd_part[h, c, :unit]
    for h in (0, 1):
        outs[h][1]()
    each(2, 3, 2, 1)
    each(0, 4)
    for i in (0, 1):
        for h in (0, 1):
            for d, step in ((0, 1), (1, -1)):
                put(gd_part.at[h, 2 * d + i, block(place(2))], gd_relay.at[h, d, i],
                    swap_send.at[1], swap_recv.at[6 + 2 * h + d], h, step)
    out_res[...] = (outs[0][2]() + outs[1][2]()).astype(BF)
    scatter(out_res, lambda r: out_back.at[pl.ds(r, slot)], back_send.at[0], back_recv.at[0])
    each(1, 4)
    for c in range(4):
        for h in (0, 1):
            for step in (1, -1):
                put(gd_part.at[h, c, block(place(step))], owned(gdown, h, 0, RING[c]),
                    swap_send.at[1], swap_recv.at[10 + h], h, step)
    each(2, 0)
    each(2, 4)
    scatter(ret_res, lambda r: ret_back.at[pl.ds(r, slot)], back_send.at[1], back_recv.at[1])
    for h in (0, 1):
        for d, step in ((0, 1), (1, -1)):
            wait_bytes(gd_relay.at[h, d], swap_recv.at[6 + 2 * h + d])
            for i in (0, 1):
                put(gd_relay.at[h, d, i], owned(gdown, h, -step, RING[2 * d + i]),
                    swap_send.at[1], swap_recv.at[10 + h], h, step)

    def home(packed, which, hot):
        return dot(dot(pack_ref[which], packed, LAST).astype(BF), hot)

    wait_bytes(out_back, back_recv.at[0])
    hot = hot_ref[...]
    scaled = out_back[...].astype(F32) * w_ref[...]
    high = scaled.astype(BF)
    low_part = (scaled - high.astype(F32)).astype(BF)
    body = pack_ref[0, :, :main]
    partial = dot(dot(body, high, LAST).astype(BF), hot) + dot(dot(body, low_part, LAST).astype(BF), hot)
    wait_bytes(ret_back, back_recv.at[1])
    grad_tok_ref[...] = home(ret_back[...], 1, hot).astype(BF)
    scaled = ret_back[:, main:].astype(F32) * w_ref[...]
    high = scaled.astype(BF)
    low_part = (scaled - high.astype(F32)).astype(BF)
    tail = pack_ref[0, :, main:]
    high = dot(tail, high, LAST).astype(BF)
    low_part = dot(tail, low_part, LAST).astype(BF)
    mixture_ref[...] = (partial + dot(high, hot) + dot(low_part, hot)).astype(BF)

    for h in (0, 1):
        wait_bytes(gd_part.at[h, pl.ds(0, 3)], swap_recv.at[10 + h])
        wait_bytes(hid_t.at[h, pl.ds(0, 3 * unit)], small_send.at[h])
        wait_bytes(gh_send.at[h], small_send.at[2 + h])
    wait_bytes(down_ring, swap_send.at[0])
    wait_bytes(gd_part, swap_send.at[1])
    wait_bytes(tok_loc.at[pl.ds(0, rows - slot)], a2a_send.at[0])
    wait_bytes(grad_loc.at[pl.ds(0, rows - slot)], a2a_send.at[1])
    wait_bytes(tok_all.at[pl.ds(0, 15)], ag_send.at[0])
    wait_bytes(grad_all.at[pl.ds(0, 6)], ag_send.at[1])
    wait_bytes(out_in, rs_send.at[0])
    wait_bytes(ret_part.at[pl.ds(0, 15)], rs_send.at[1])
    wait_bytes(out_res.at[pl.ds(0, rows - slot)], back_send.at[0])
    wait_bytes(ret_res.at[pl.ds(0, rows - slot)], back_send.at[1])


def finish_kernel(*refs):
    n = len(refs) // 2
    stores = [pltpu.make_async_copy(refs[i], refs[n + i], refs[-1].at[i]) for i in range(n)]
    for store in stores:
        store.start()
    for store in stores:
        store.wait()


def per_device(tokens, cotangent, gate_weight, up_weight, down_weight, chosen, counts, gate_prob):
    experts, _, slots = chosen.shape
    n_tok, feats = tokens.shape
    rows = experts * slots
    width = gate_weight.shape[1]
    hidden = gate_weight.shape[2]
    wide, main = 512, 384
    n = width // feats
    vmem = pl.BlockSpec(memory_space=pltpu.VMEM)
    smem = pl.BlockSpec(memory_space=pltpu.SMEM)
    hbm = pl.BlockSpec(memory_space=pl.ANY)
    dma = pltpu.SemaphoreType.DMA
    half = rows // 2
    kept = pl.pallas_call(
        kernel,
        out_shape=(
            pltpu.VMEM((feats, n_tok), BF),
            pltpu.VMEM((feats, n_tok), BF),
            pltpu.VMEM((width, hidden), BF),
            pltpu.VMEM((width, hidden), BF),
            pltpu.VMEM((hidden, width), BF),
        ),
        in_specs=[smem] + [vmem] * 4 + [hbm] * 3,
        out_specs=(vmem,) * 5,
        scratch_shapes=[
            pltpu.VMEM((rows, main), BF),
            pltpu.VMEM((rows, wide), BF),
            pltpu.VMEM((rows, n_tok), BF),
            pltpu.VMEM((rows, 1), F32),
            pltpu.VMEM((2, feats, wide), BF),
            pltpu.VMEM((rows, wide), BF),
            pltpu.VMEM((rows, main), BF),
            pltpu.VMEM((n, rows, wide), BF),
            pltpu.VMEM((n, rows, main), BF),
            pltpu.VMEM((n // 2, rows, 128), BF),
            pltpu.VMEM((n // 2, rows, 128), BF),
            pltpu.VMEM((width, hidden), BF),
            pltpu.VMEM((width, hidden), BF),
            pltpu.VMEM((hidden, width), BF),
            pltpu.VMEM((2, 4, 256, main), BF),
            pltpu.VMEM((2, 2, 2, 64, main), BF),
            pltpu.VMEM((2, 4, 256, main), BF),
            pltpu.VMEM((2, 2, 2, 64, main), BF),
            pltpu.VMEM((rows, hidden), BF),
            pltpu.VMEM((2, 256, rows), BF),
            pltpu.VMEM((2, rows, 256), BF),
            pltpu.VMEM((2, 192, rows), BF),
            pltpu.VMEM((hidden, rows), F32),
            pltpu.VMEM((2, 3, 64, rows), BF),
            pltpu.VMEM((rows, 2 * hidden), F32),
            pltpu.VMEM((rows, 2 * hidden), BF),
            pltpu.VMEM((2, 4, rows, main), BF),
            pltpu.VMEM((n, rows, wide), BF),
            pltpu.VMEM((2, 3 * rows, main), BF),
            pltpu.VMEM((2, 4, 3 * half, wide), BF),
            pltpu.VMEM((2, 3 * half, wide), BF),
            pltpu.VMEM((rows, main), BF),
            pltpu.VMEM((rows, wide), BF),
            dma((3,)),
            dma((2,)),
            dma((3,)),
            dma((2,)),
            dma((48,)),
            dma((2,)),
            dma((60,)),
            dma((12,)),
            dma((2,)),
            dma((2,)),
            dma((2,)),
            dma((12,)),
            dma((4,)),
            dma((4,)),
        ],
        compiler_params=pltpu.CompilerParams(
            collective_id=0, has_side_effects=True, vmem_limit_bytes=52 * 1024 * 1024
        ),
        name="experts",
    )(
        counts[:, 0],
        chosen[:, 0, :],
        gate_prob[:, 0, :],
        tokens.T,
        cotangent.T,
        gate_weight[0],
        up_weight[0],
        down_weight[0],
    )
    mixture, grad_tokens, grad_gate, grad_up, grad_down = pl.pallas_call(
        finish_kernel,
        out_shape=(
            jax.ShapeDtypeStruct((feats, n_tok), BF),
            jax.ShapeDtypeStruct((feats, n_tok), BF),
            jax.ShapeDtypeStruct((width, hidden), BF),
            jax.ShapeDtypeStruct((width, hidden), BF),
            jax.ShapeDtypeStruct((hidden, width), BF),
        ),
        in_specs=[vmem] * 5,
        out_specs=(hbm,) * 5,
        scratch_shapes=[dma((5,))],
        compiler_params=pltpu.CompilerParams(vmem_limit_bytes=16 * 1024 * 1024),
        name="finish",
    )(*kept)
    return mixture.T, grad_tokens.T, grad_gate[None], grad_up[None], grad_down[None]


def solution(mesh):
    placed = (
        P("ep", "fsdp"),
        P("ep", "fsdp"),
        P("ep", None, "fsdp"),
        P("ep", None, "fsdp"),
        P("ep", "fsdp", None),
        P(None, "ep", None),
        P(None, "ep"),
        P(None, "ep", None),
    )
    return jax.shard_map(
        per_device,
        mesh=mesh,
        in_specs=placed,
        out_specs=(
            P("ep", "fsdp"),
            P("ep", "fsdp"),
            P("ep", None, "fsdp"),
            P("ep", None, "fsdp"),
            P("ep", "fsdp", None),
        ),
        check_vma=False,
    )
```

```python
import jax
import jax.numpy as jnp
from jax import lax
from jax.experimental import pallas as pl
from jax.experimental.pallas import tpu as pltpu
from jax.sharding import PartitionSpec as P

MESH = pl.DeviceIdType.MESH
BF = jnp.bfloat16
F32 = jnp.float32
SIDE = 4
RING = (0, -1, 1, 2)
LAST = (((1,), (1,)), ((), ()))
ROWS = (((0,), (0,)), ((), ()))


def dot(a, b, dims=(((1,), (0,)), ((), ()))):
    return lax.dot_general(a, b, dims, preferred_element_type=F32)


def packings(odd, feats, main, wide):
    fi = lax.broadcasted_iota(jnp.int32, (feats, main), 0)
    fj = lax.broadcasted_iota(jnp.int32, (feats, main), 1)
    body = jnp.where(fi - fj == 64 * odd, 1.0, 0.0)
    ti = lax.broadcasted_iota(jnp.int32, (feats, wide - main), 0)
    tj = lax.broadcasted_iota(jnp.int32, (feats, wide - main), 1)
    where = jnp.where(odd == 1, ti, ti - main)

    def packing(low):
        tail = jnp.where((tj - where == low) & (tj >= low) & (tj < low + 64), 1.0, 0.0)
        return jnp.concatenate([body, tail], axis=1).astype(BF)

    return packing(64 * odd), packing(64 - 64 * odd)


def kernel(
    count_ref, chosen_ref, prob_ref, tok_hbm, cot_hbm, gate_hbm, up_hbm, down_hbm,
    mixture_ref, grad_tok_ref, ggate, gup, gdown,
    tok_ref, cot_ref, out_back, ret_back, hot_ref, w_ref, pack_ref,
    tok_loc, grad_loc, tok_all, grad_all, tok_rem, grad_rem,
    gate, up, down, down_ring, down_relay, gd_part, gd_relay,
    hid, hid_t, hid_g, gh_send, gh_own, gh_in, pre, gpre,
    out_part, ret_part, out_in, ret_in, ret_in2, out_res, ret_res,
    w_sem, a2a_send, a2a_recv, ag_send, ag_recv, rs_send, rs_recv, out_recv, back_send, back_recv,
    swap_send, swap_recv, small_send, small_recv,
):
    f = lax.axis_index("fsdp")
    me = lax.axis_index("ep")
    n_ep = chosen_ref.shape[0]
    y = lax.div(f, SIDE)
    x = lax.rem(f, SIDE)
    odd = lax.rem(x, 2)
    wide = tok_all.shape[2]
    main = grad_all.shape[2]
    rows = tok_all.shape[1]
    half = rows // 2
    n_seg = 2
    seg = rows // n_seg
    piece = seg // 2
    bit = seg // 4
    feats = tok_ref.shape[0]
    pair = 2 * feats
    slot = 16
    unit = 64

    def flat(dy, dx):
        return lax.rem(y + dy + SIDE, SIDE) * SIDE + lax.rem(x + dx + SIDE, SIDE)

    def coord(axis, along, other=0):
        return (other, along) if axis == 0 else (along, other)

    def place(o):
        return RING.index(o)

    barrier = pltpu.get_barrier_semaphore()
    for axis in (0, 1):
        for o in (1, -1, 2):
            pl.semaphore_signal(barrier, inc=1, device_id={"fsdp": flat(*coord(axis, o))}, device_id_type=MESH)

    @pl.loop(1, n_ep)
    def _(k):
        pl.semaphore_signal(barrier, inc=1, device_id={"ep": lax.rem(me + k, n_ep)}, device_id_type=MESH)

    loads = [
        pltpu.make_async_copy(src, dst, w_sem.at[i])
        for i, (src, dst) in enumerate(
            ((down_hbm, down), (gate_hbm, gate), (up_hbm, up), (tok_hbm, tok_ref), (cot_hbm, cot_ref))
        )
    ]
    for i in (0, 3, 4, 1, 2):
        loads[i].start()

    def wait_bytes(ref, sem):
        pltpu.make_async_copy(ref, ref, sem).wait()

    def put(src, dst, send, recv, axis, step):
        pltpu.make_async_remote_copy(
            src_ref=src, dst_ref=dst, send_sem=send, recv_sem=recv,
            device_id={"fsdp": flat(*coord(axis, step))}, device_id_type=MESH,
        ).start()

    def lanes(h, along, other):
        slice_ = flat(*coord(h, along, other))
        first = pair * lax.div(slice_, 2) + wide * lax.rem(slice_, 2)
        return pl.ds(pl.multiple_of(first, 128), main)

    def owned(ref, h, along, other):
        return ref.at[pl.ds(h * unit, unit), lanes(h, along, other)]

    def block(i):
        return pl.ds(i * unit, unit)

    loads[0].wait()
    pl.semaphore_wait(barrier, n_ep + 5)

    for i in (0, 1):
        for h in (0, 1):
            for d, step in ((0, 1), (1, -1)):
                put(owned(down, h, 2, RING[2 * d + i]), down_relay.at[h, d, i],
                    swap_send.at[0], swap_recv.at[2 * h + d], h, step)
    for c in range(4):
        for h in (0, 1):
            for step in (1, -1):
                put(owned(down, h, step, RING[c]), down_ring.at[h, c, block(place(-step))],
                    swap_send.at[0], swap_recv.at[4 + h], h, step)


    n_tok = tok_ref.shape[1]
    pack_a, pack_b = packings(odd, feats, main, wide)
    pack_ref[0] = pack_a
    pack_ref[1] = pack_b
    j = lax.broadcasted_iota(jnp.int32, (1, slot), 1)
    index, weight = [], []
    for e in range(n_ep):
        live = j < count_ref[e]
        index.append(jnp.broadcast_to(jnp.where(live, chosen_ref[e : e + 1], -1), (slot, slot)))
        weight.append(jnp.broadcast_to(jnp.where(live, prob_ref[e : e + 1], 0.0), (slot, slot)))
    shape = (rows, slot)
    mine = lax.rem(lax.broadcasted_iota(jnp.int32, shape, 0), slot) == lax.broadcasted_iota(jnp.int32, shape, 1)
    index = jnp.concatenate(index, axis=0).astype(F32)
    index = jnp.sum(jnp.where(mine, index, 0.0), axis=1, keepdims=True).astype(jnp.int32)
    weight = jnp.concatenate(weight, axis=0)
    w_ref[...] = jnp.sum(jnp.where(mine, weight, 0.0), axis=1, keepdims=True)
    hit = lax.broadcasted_iota(jnp.int32, (rows, n_tok), 1) == index
    onehot = jnp.where(hit, 1.0, 0.0).astype(BF)
    hot_ref[...] = onehot

    loads[3].wait()
    loads[4].wait()
    tp = dot(dot(onehot, tok_ref[...], LAST).astype(BF), pack_a)
    gp = dot((dot(onehot, cot_ref[...], LAST) * w_ref[...]).astype(BF), pack_b)
    tok_loc[:, :main] = tp[:, :main].astype(BF)
    tok_loc[:, main:] = (tp[:, main:] + gp[:, main:]).astype(BF)
    grad_loc[...] = gp[:, :main].astype(BF)

    def scatter(src, dst_of, send, recv):
        @pl.loop(0, n_ep - 1)
        def _(t):
            gap = lax.div(t + 1, 2) * (1 - 2 * lax.rem(t, 2))
            peer = lax.rem(me + n_ep // 2 + gap, n_ep)
            pltpu.make_async_remote_copy(
                src_ref=src.at[pl.ds(peer * slot, slot)],
                dst_ref=dst_of(me * slot),
                send_sem=send,
                recv_sem=recv,
                device_id={"ep": peer},
                device_id_type=MESH,
            ).start()

        pltpu.make_async_copy(src.at[pl.ds(me * slot, slot)], dst_of(me * slot), recv).start()

    part = lax.div(me, n_ep // 2)
    scatter(grad_loc, lambda r: grad_all.at[f, pl.ds(r, slot)], a2a_send.at[1], a2a_recv.at[2])
    scatter(tok_loc, lambda r: tok_all.at[f, pl.ds(r, slot)], a2a_send.at[0], a2a_recv.at[part])

    def swap_relay():
        for h in (0, 1):
            for d, step in ((0, 1), (1, -1)):
                wait_bytes(down_relay.at[h, d], swap_recv.at[2 * h + d])
                for i in (0, 1):
                    put(down_relay.at[h, d, i], down_ring.at[h, 2 * d + i, block(place(2))],
                        swap_send.at[0], swap_recv.at[4 + h], h, step)

    for h in (0, 1):
        for c in range(4):
            down_ring[h, c, :unit] = down[h * unit : (h + 1) * unit, lanes(h, 0, RING[c])]
    swap_relay()

    def gather(buf, send, g):
        def sem(h, i):
            return ag_recv.at[g * 40 + h * 20 + i]

        def ref(h, fst, snd, q=None):
            o = coord(h, fst, snd)
            first = g * seg + h * piece + (0 if q is None else q * bit)
            return buf.at[flat(*o), pl.ds(first, piece if q is None else bit)]

        def wait(h, i, fst, snd, q=None):
            wait_bytes(ref(h, fst, snd, q), sem(h, i))

        def send_block(h, i, fst, snd, axis, step, q=None):
            r = ref(h, fst, snd, q)
            put(r, r, send, sem(h, i), axis, step)

        def own(h):
            for i, step in ((0, 1), (1, -1)):
                send_block(h, i, 0, 0, h, step)
            for i, step in ((4, 1), (5, -1)):
                send_block(h, i, 0, 0, 1 - h, step)

        def spread(h, j):
            for i, step in ((0, 1), (1, -1)):
                send_block(h, 4 + 4 * j + i, RING[j], 0, 1 - h, step)

        def s1():
            for i in (0, 1):
                o = (-1, 1)[i]
                for h in (0, 1):
                    wait(h, i, o, 0)
                    send_block(h, 2 + i, o, 0, h, -o, i)
                for h in (0, 1):
                    spread(h, 1 + i)

        def relay(j):
            for i in (0, 1):
                o = (-1, 1)[i]
                for h in (1, 0):
                    wait(h, 4 + 4 * j + i, RING[j], o)
                    send_block(h, 6 + 4 * j + i, RING[j], o, 1 - h, -o, i)

        def s3():
            for h in (0, 1):
                wait(h, 2, 2, 0, 0)
                wait(h, 3, 2, 0, 1)
                spread(h, 3)

        def finish():
            for j in range(4):
                for h in (0, 1):
                    for i in (0, 1):
                        wait(h, 6 + 4 * j + i, RING[j], 2, i)

        return own, s1, relay, s3, finish

    def ring(axis, term, land, n, sem, send):
        q1, q2, fp, fm = 0, n, 2 * n, 4 * n

        def init():
            put(term(2, 0), land(q1, n), send, sem(0), axis, 1)
            put(term(2, 1), land(q2, n), send, sem(1), axis, -1)
            put(term(1, 1), land(fp + n, n), send, sem(2), axis, 1)
            put(term(-1, 0), land(fm, n), send, sem(3), axis, -1)

        def comb():
            for i, k, first, dst in ((0, 1, q1, fp), (1, -1, q2, fm + n)):
                r = land(first, n)
                wait_bytes(r, sem(i))
                r[...] = (r[...].astype(F32) + term(k, i)[...].astype(F32)).astype(BF)
                put(r, land(dst, n), send, sem(4 + i), axis, k)

        def total():
            for first, i in ((fp + n, 2), (fm, 3), (fp, 4), (fm + n, 5)):
                wait_bytes(land(first, n), sem(i))
            return (
                term(0)[...].astype(F32)
                + land(fp, 2 * n)[...].astype(F32)
                + land(fm, 2 * n)[...].astype(F32)
            )

        return init, comb, total

    def reduce(buf, in1, in2, res, send, g):
        def make(h, j):
            def term(k, q=None):
                o = coord(h, RING[j], k) if j < 4 else coord(h, k, 0)
                first = g * seg + h * piece + (0 if q is None else q * bit)
                return buf.at[flat(*o), pl.ds(first, piece if q is None else bit)]

            def land(first, n):
                if j < 4:
                    return in1.at[g, h, j, pl.ds(first, n)]
                return in2.at[g, h, pl.ds(first, n)]

            def sem(i):
                return rs_recv.at[g * 60 + h * 30 + j * 6 + i]

            init, comb, total = ring(1 - h if j < 4 else h, term, land, bit, sem, send)

            def fin():
                if j < 4:
                    term(0)[...] = total().astype(BF)
                else:
                    res[pl.ds(g * seg + h * piece, piece)] = total().astype(BF)

            return init, comb, fin

        return {(h, j): make(h, j) for h in (0, 1) for j in range(5)}

    def grad_block(axis, o, q=None):
        g = grad_all.at[flat(*coord(axis, o))]
        return g if q is None else g.at[pl.ds(q * half, half)]

    def grad_sem(axis, i):
        return ag_recv.at[n_seg * 40 + axis * 4 + i]

    wait_bytes(grad_all.at[f], a2a_recv.at[2])
    for axis in (0, 1):
        for i, step in ((0, 1), (1, -1)):
            put(grad_block(axis, 0), grad_block(axis, 0), ag_send.at[1], grad_sem(axis, i), axis, step)
    tree = [gather(tok_all, ag_send.at[0], g) for g in range(n_seg)]
    own, s1, relay, s3, finish = zip(*tree)
    for g in range(n_seg):
        wait_bytes(tok_all.at[f, pl.ds(g * seg, seg)], a2a_recv.at[g])
        for h in (0, 1):
            own[g](h)
    for i in (0, 1):
        o = (-1, 1)[i]
        for axis in (0, 1):
            wait_bytes(grad_block(axis, o), grad_sem(axis, i))
            put(grad_block(axis, o, i), grad_block(axis, o, i), ag_send.at[1], grad_sem(axis, 2 + i), axis, -o)
    s1[0]()

    def grad_hidden(h):
        wait_bytes(down_ring.at[h, pl.ds(0, 3)], swap_recv.at[4 + h])
        for i in (0, 1):
            wait_bytes(grad_block(1 - h, 2, i), grad_sem(1 - h, 2 + i))
        term = jnp.zeros((4 * unit, rows), F32)
        for c in range(4):
            term = term + dot(down_ring[h, c], grad_block(1 - h, RING[c])[...], LAST)
        gh_own[pl.ds(h * unit, unit)] = term[:unit]
        gh_send[h] = term[unit:].astype(BF)
        for o in (2, 1, -1):
            put(gh_send.at[h, block(place(o) - 1)], gh_in.at[h, place(-o if o < 2 else 2) - 1],
                small_send.at[2 + h], small_recv.at[2 + h], h, o)

    grad_hidden(0)
    relay[0](0)
    s3[0]()
    grad_hidden(1)
    relay[0](1)
    relay[0](2)
    s1[1]()
    relay[0](3)
    n_pair = tok_all.shape[0] // 2
    low = lax.broadcasted_iota(jnp.int32, (seg, 128), 1) < 64

    def span(p, size=pair):
        return pl.ds(pl.multiple_of(p * pair, 128), size)

    def rest(p):
        return pl.ds(pl.multiple_of(p * pair + main, 128), 128)

    def tok_pair(p, r=slice(None)):
        return jnp.concatenate(
            [tok_all[2 * p, r, :main], tok_rem[p, r], tok_all[2 * p + 1, r, :main]], axis=1
        )

    def row_at(d):
        return lax.rem(y + d, SIDE)

    def accumulate(p, g):
        r = pl.ds(g * seg, seg)
        even = tok_all[2 * p, r, main:].astype(F32)
        other = tok_all[2 * p + 1, r, main:].astype(F32)
        tok_rem[p, r] = jnp.where(low, even, other).astype(BF)
        grad_rem[p, r] = pltpu.roll(jnp.where(low, other, even), 64, 1).astype(BF)
        both = jnp.concatenate([gate[span(p)], up[span(p)]], axis=1)
        pre[r] += dot(tok_pair(p, r), both)
        gh_own[:, r] += dot(down[:, rest(p)], grad_rem[p, r], LAST)

    pre[...] = jnp.zeros_like(pre)
    loads[1].wait()
    loads[2].wait()
    for h in (0, 1):
        wait_bytes(gh_in.at[h], small_recv.at[2 + h])
        gh_own[pl.ds(h * unit, unit)] += (
            gh_in[h, 0].astype(F32) + gh_in[h, 1].astype(F32) + gh_in[h, 2].astype(F32)
        )
    relay[1](0)
    s3[1]()
    relay[1](1)
    relay[1](2)
    xp = lax.div(x, 2)
    rets = [reduce(ret_part, ret_in, ret_in2, ret_res, rs_send.at[1], g) for g in range(n_seg)]

    def each(g, step, *order):
        for j in order:
            for h in (0, 1):
                rets[g][h, j][step]()

    def forward(g):
        finish[g]()

        @pl.loop(0, n_pair)
        def _(p):
            accumulate(p, g)

    def turn(g):
        r = pl.ds(g * seg, seg)
        pg = pre[r, :128]
        pu = pre[r, 128:]
        sg = jax.nn.sigmoid(pg)
        hid[r] = (pg * sg * pu).astype(BF)
        gh = jnp.transpose(gh_own[:, g * seg : (g + 1) * seg])
        gpre[r, :128] = (gh * pu * sg * (1.0 + pg * (1.0 - sg))).astype(BF)
        gpre[r, 128:] = (gh * (pg * sg)).astype(BF)

    def ret_pair(p, g):
        r = pl.ds(g * seg, seg)
        both = jnp.concatenate([gate[span(p)], up[span(p)]], axis=1)
        t = dot(gpre[r], both, LAST)
        ret_part[2 * p, r, :main] = t[:, :main].astype(BF)
        ret_part[2 * p + 1, r, :main] = t[:, wide:].astype(BF)
        rem = pltpu.roll(t[:, main:wide], 64, 1)
        o = dot(hid[r], down[:, rest(p)])
        ret_part[2 * p, r, main:] = jnp.where(low, o, rem).astype(BF)
        ret_part[2 * p + 1, r, main:] = jnp.where(low, rem, o).astype(BF)

    def back(g):
        @pl.loop(0, 2)
        def _(t):
            ret_pair(2 * row_at(2) + t, g)

        rets[g][1, 3][0]()

        @pl.loop(3, 6)
        def _(t):
            ret_pair(2 * row_at(t) + 1 - xp, g)

        rets[g][0, 3][0]()

        @pl.loop(3, 6)
        def _(t):
            ret_pair(2 * row_at(t) + xp, g)

        each(g, 0, 2, 1, 0)

    forward(0)
    relay[1](3)
    turn(0)
    back(0)
    forward(1)
    turn(1)
    turned = jnp.transpose(hid[...].astype(F32)).astype(BF)
    for h in (0, 1):
        hid_t[h, :unit] = turned[h * unit : (h + 1) * unit]
    for o in (2, 1, -1):
        for h in (0, 1):
            put(hid_t.at[h, block(0)], hid_t.at[h, block(place(-o if o < 2 else 2))],
                small_send.at[h], small_recv.at[h], h, o)
    back(1)
    each(0, 1, 3, 2)

    outs = []
    for h in (0, 1):
        wait_bytes(hid_t.at[h, pl.ds(0, 3 * unit)], small_recv.at[h])
        hid_g[h] = jnp.transpose(hid_t[h].astype(F32)).astype(BF)
        for c in range(4):
            out_part[h, c] = dot(hid_g[h], down_ring[h, c]).astype(BF)

        def term(k, q=None, h=h):
            r = out_part.at[h, place(k)]
            return r if q is None else r.at[pl.ds(q * half, half)]

        def land(first, n, h=h):
            return out_in.at[h, pl.ds(first, n)]

        outs.append(ring(1 - h, term, land, half, lambda i, h=h: out_recv.at[h * 6 + i], rs_send.at[0]))
        outs[h][0]()
    each(0, 1, 1, 0)
    for h in (0, 1):
        outs[h][1]()
    each(1, 1, 3, 2)
    for h in (0, 1):
        for c in range(4):
            gd_part[h, c] = dot(hid_t[h], grad_block(1 - h, RING[c])[...]).astype(BF)
            gdown[h * unit : (h + 1) * unit, lanes(h, 0, RING[c])] = gd_part[h, c, :unit]
    each(0, 2, 3, 2, 1)
    each(0, 0, 4)
    each(1, 1, 1, 0)

    @pl.loop(0, n_pair)
    def _(p):
        g = dot(tok_pair(p), gpre[...], ROWS).astype(BF)
        ggate[span(p)] = g[:, :128]
        gup[span(p)] = g[:, 128:]
        gdown[:, rest(p)] = dot(hid[...], grad_rem[p], ROWS).astype(BF)

    out_res[...] = (outs[0][2]() + outs[1][2]()).astype(BF)
    scatter(out_res, lambda r: out_back.at[pl.ds(r, slot)], back_send.at[0], back_recv.at[0])
    each(0, 1, 4)
    each(1, 2, 3, 2, 1)
    each(1, 0, 4)
    for i in (0, 1):
        for h in (0, 1):
            for d, step in ((0, 1), (1, -1)):
                put(gd_part.at[h, 2 * d + i, block(place(2))], gd_relay.at[h, d, i],
                    swap_send.at[1], swap_recv.at[6 + 2 * h + d], h, step)

    def ret_home(g):
        each(g, 2, 0)
        each(g, 2, 4)
        n_part = n_ep // n_seg
        there = ret_back.at[pl.ds(me * slot, slot)]

        @pl.loop(0, n_part)
        def _(t):
            peer = g * n_part + lax.rem(me + n_part // 2 + t, n_part)

            @pl.when(peer != me)
            def _():
                pltpu.make_async_remote_copy(
                    src_ref=ret_res.at[pl.ds(peer * slot, slot)],
                    dst_ref=there,
                    send_sem=back_send.at[1],
                    recv_sem=back_recv.at[1],
                    device_id={"ep": peer},
                    device_id_type=MESH,
                ).start()

            @pl.when(peer == me)
            def _():
                pltpu.make_async_copy(ret_res.at[pl.ds(me * slot, slot)], there, back_recv.at[1]).start()

    ret_home(0)
    each(1, 1, 4)
    for c in range(4):
        for h in (0, 1):
            for step in (1, -1):
                put(gd_part.at[h, c, block(place(step))], owned(gdown, h, 0, RING[c]),
                    swap_send.at[1], swap_recv.at[10 + h], h, step)
    ret_home(1)
    for h in (0, 1):
        for d, step in ((0, 1), (1, -1)):
            wait_bytes(gd_relay.at[h, d], swap_recv.at[6 + 2 * h + d])
            for i in (0, 1):
                put(gd_relay.at[h, d, i], owned(gdown, h, -step, RING[2 * d + i]),
                    swap_send.at[1], swap_recv.at[10 + h], h, step)

    def home(packed, which, hot):
        return dot(dot(pack_ref[which], packed, LAST).astype(BF), hot)

    wait_bytes(out_back, back_recv.at[0])
    hot = hot_ref[...]
    scaled = out_back[...].astype(F32) * w_ref[...]
    high = scaled.astype(BF)
    low_part = (scaled - high.astype(F32)).astype(BF)
    body = pack_ref[0, :, :main]
    partial = dot(dot(body, high, LAST).astype(BF), hot) + dot(dot(body, low_part, LAST).astype(BF), hot)
    wait_bytes(ret_back, back_recv.at[1])
    grad_tok_ref[...] = home(ret_back[...], 1, hot).astype(BF)
    scaled = ret_back[:, main:].astype(F32) * w_ref[...]
    high = scaled.astype(BF)
    low_part = (scaled - high.astype(F32)).astype(BF)
    tail = pack_ref[0, :, main:]
    high = dot(tail, high, LAST).astype(BF)
    low_part = dot(tail, low_part, LAST).astype(BF)
    mixture_ref[...] = (partial + dot(high, hot) + dot(low_part, hot)).astype(BF)

    for h in (0, 1):
        wait_bytes(gd_part.at[h, pl.ds(0, 3)], swap_recv.at[10 + h])
        wait_bytes(hid_t.at[h, pl.ds(0, 3 * unit)], small_send.at[h])
        wait_bytes(gh_send.at[h], small_send.at[2 + h])
    wait_bytes(down_ring, swap_send.at[0])
    wait_bytes(gd_part, swap_send.at[1])
    wait_bytes(tok_loc.at[pl.ds(0, rows - slot)], a2a_send.at[0])
    wait_bytes(grad_loc.at[pl.ds(0, rows - slot)], a2a_send.at[1])
    wait_bytes(tok_all.at[pl.ds(0, 15)], ag_send.at[0])
    wait_bytes(grad_all.at[pl.ds(0, 6)], ag_send.at[1])
    wait_bytes(out_in, rs_send.at[0])
    wait_bytes(ret_part.at[pl.ds(0, 15)], rs_send.at[1])
    wait_bytes(out_res.at[pl.ds(0, rows - slot)], back_send.at[0])
    wait_bytes(ret_res.at[pl.ds(0, rows - slot)], back_send.at[1])


def finish_kernel(*refs):
    n = len(refs) // 2
    stores = [pltpu.make_async_copy(refs[i], refs[n + i], refs[-1].at[i]) for i in range(n)]
    for store in stores:
        store.start()
    for store in stores:
        store.wait()


def per_device(tokens, cotangent, gate_weight, up_weight, down_weight, chosen, counts, gate_prob):
    experts, _, slots = chosen.shape
    n_tok, feats = tokens.shape
    rows = experts * slots
    width = gate_weight.shape[1]
    hidden = gate_weight.shape[2]
    wide, main = 512, 384
    n = width // feats
    vmem = pl.BlockSpec(memory_space=pltpu.VMEM)
    smem = pl.BlockSpec(memory_space=pltpu.SMEM)
    hbm = pl.BlockSpec(memory_space=pl.ANY)
    dma = pltpu.SemaphoreType.DMA
    half = rows // 2
    kept = pl.pallas_call(
        kernel,
        out_shape=(
            pltpu.VMEM((feats, n_tok), BF),
            pltpu.VMEM((feats, n_tok), BF),
            pltpu.VMEM((width, hidden), BF),
            pltpu.VMEM((width, hidden), BF),
            pltpu.VMEM((hidden, width), BF),
        ),
        in_specs=[smem] + [vmem] * 2 + [hbm] * 5,
        out_specs=(vmem,) * 5,
        scratch_shapes=[
            pltpu.VMEM((feats, n_tok), BF),
            pltpu.VMEM((feats, n_tok), BF),
            pltpu.VMEM((rows, main), BF),
            pltpu.VMEM((rows, wide), BF),
            pltpu.VMEM((rows, n_tok), BF),
            pltpu.VMEM((rows, 1), F32),
            pltpu.VMEM((2, feats, wide), BF),
            pltpu.VMEM((rows, wide), BF),
            pltpu.VMEM((rows, main), BF),
            pltpu.VMEM((n, rows, wide), BF),
            pltpu.VMEM((n, rows, main), BF),
            pltpu.VMEM((n // 2, rows, 128), BF),
            pltpu.VMEM((n // 2, rows, 128), BF),
            pltpu.VMEM((width, hidden), BF),
            pltpu.VMEM((width, hidden), BF),
            pltpu.VMEM((hidden, width), BF),
            pltpu.VMEM((2, 4, 256, main), BF),
            pltpu.VMEM((2, 2, 2, 64, main), BF),
            pltpu.VMEM((2, 4, 256, main), BF),
            pltpu.VMEM((2, 2, 2, 64, main), BF),
            pltpu.VMEM((rows, hidden), BF),
            pltpu.VMEM((2, 256, rows), BF),
            pltpu.VMEM((2, rows, 256), BF),
            pltpu.VMEM((2, 192, rows), BF),
            pltpu.VMEM((hidden, rows), F32),
            pltpu.VMEM((2, 3, 64, rows), BF),
            pltpu.VMEM((rows, 2 * hidden), F32),
            pltpu.VMEM((rows, 2 * hidden), BF),
            pltpu.VMEM((2, 4, rows, main), BF),
            pltpu.VMEM((n, rows, wide), BF),
            pltpu.VMEM((2, 3 * rows, main), BF),
            pltpu.VMEM((2, 2, 4, 3 * half // 2, wide), BF),
            pltpu.VMEM((2, 2, 3 * half // 2, wide), BF),
            pltpu.VMEM((rows, main), BF),
            pltpu.VMEM((rows, wide), BF),
            dma((5,)),
            dma((2,)),
            dma((3,)),
            dma((2,)),
            dma((88,)),
            dma((2,)),
            dma((120,)),
            dma((12,)),
            dma((2,)),
            dma((2,)),
            dma((2,)),
            dma((12,)),
            dma((4,)),
            dma((4,)),
        ],
        compiler_params=pltpu.CompilerParams(
            collective_id=0, has_side_effects=True, vmem_limit_bytes=52 * 1024 * 1024
        ),
        name="experts",
    )(
        counts[:, 0],
        chosen[:, 0, :],
        gate_prob[:, 0, :],
        tokens.T,
        cotangent.T,
        gate_weight[0],
        up_weight[0],
        down_weight[0],
    )
    mixture, grad_tokens, grad_gate, grad_up, grad_down = pl.pallas_call(
        finish_kernel,
        out_shape=(
            jax.ShapeDtypeStruct((feats, n_tok), BF),
            jax.ShapeDtypeStruct((feats, n_tok), BF),
            jax.ShapeDtypeStruct((width, hidden), BF),
            jax.ShapeDtypeStruct((width, hidden), BF),
            jax.ShapeDtypeStruct((hidden, width), BF),
        ),
        in_specs=[vmem] * 5,
        out_specs=(hbm,) * 5,
        scratch_shapes=[dma((5,))],
        compiler_params=pltpu.CompilerParams(vmem_limit_bytes=16 * 1024 * 1024),
        name="finish",
    )(*kept)
    return mixture.T, grad_tokens.T, grad_gate[None], grad_up[None], grad_down[None]


def solution(mesh):
    placed = (
        P("ep", "fsdp"),
        P("ep", "fsdp"),
        P("ep", None, "fsdp"),
        P("ep", None, "fsdp"),
        P("ep", "fsdp", None),
        P(None, "ep", None),
        P(None, "ep"),
        P(None, "ep", None),
    )
    return jax.shard_map(
        per_device,
        mesh=mesh,
        in_specs=placed,
        out_specs=(
            P("ep", "fsdp"),
            P("ep", "fsdp"),
            P("ep", None, "fsdp"),
            P("ep", None, "fsdp"),
            P("ep", "fsdp", None),
        ),
        check_vma=False,
    )
```

```python
import jax
import jax.numpy as jnp
from jax import lax
from jax.experimental import pallas as pl
from jax.experimental.pallas import tpu as pltpu
from jax.sharding import PartitionSpec as P

MESH = pl.DeviceIdType.MESH
BF = jnp.bfloat16
F32 = jnp.float32
SIDE = 4
RING = (0, -1, 1, 2)
LAST = (((1,), (1,)), ((), ()))
ROWS = (((0,), (0,)), ((), ()))


def dot(a, b, dims=(((1,), (0,)), ((), ()))):
    return lax.dot_general(a, b, dims, preferred_element_type=F32)


def kernel(
    count_ref, chosen_ref, prob_ref, tok_hbm, cot_hbm, gate_hbm, up_hbm, down_hbm,
    mixture_ref, grad_tok_ref, ggate, gup, gdown,
    tok_ref, cot_ref, out_back, ret_back, hot_ref, w_ref, mix_t,
    tok_loc, grad_loc, tok_all, grad_all, tok_rem, grad_rem,
    gate, up, down, down_ring, down_relay, gd_part, gd_relay,
    hid, hid_t, hid_g, gh_send, gh_own, gh_in, pre, gpre,
    out_part, ret_part, out_in, ret_in, ret_in2, out_res, ret_res,
    w_sem, a2a_send, a2a_recv, ag_send, ag_recv, rs_send, rs_recv, out_recv, back_send, back_recv,
    swap_send, swap_recv, small_send, small_recv,
):
    f = lax.axis_index("fsdp")
    me = lax.axis_index("ep")
    n_ep = chosen_ref.shape[0]
    y = lax.div(f, SIDE)
    x = lax.rem(f, SIDE)
    odd = lax.rem(x, 2)
    wide = tok_all.shape[2]
    main = grad_all.shape[2]
    rows = tok_all.shape[1]
    half = rows // 2
    n_seg = 2
    seg = rows // n_seg
    piece = seg // 2
    bit = seg // 4
    feats = tok_hbm.shape[0]
    pair = 2 * feats
    slot = 16
    unit = 64

    def flat(dy, dx):
        return lax.rem(y + dy + SIDE, SIDE) * SIDE + lax.rem(x + dx + SIDE, SIDE)

    def coord(axis, along, other=0):
        return (other, along) if axis == 0 else (along, other)

    def place(o):
        return RING.index(o)

    barrier = pltpu.get_barrier_semaphore()
    for axis in (0, 1):
        for o in (1, -1, 2):
            pl.semaphore_signal(barrier, inc=1, device_id={"fsdp": flat(*coord(axis, o))}, device_id_type=MESH)

    @pl.loop(1, n_ep)
    def _(k):
        pl.semaphore_signal(barrier, inc=1, device_id={"ep": lax.rem(me + k, n_ep)}, device_id_type=MESH)

    loads = [
        pltpu.make_async_copy(src, dst, w_sem.at[i])
        for i, (src, dst) in enumerate(
            ((down_hbm, down), (gate_hbm, gate), (up_hbm, up), (tok_hbm, tok_ref.at[pl.ds(0, tok_hbm.shape[0])]),
             (cot_hbm, cot_ref.at[pl.ds(0, tok_hbm.shape[0])]))
        )
    ]
    for i in (0, 3, 4, 1, 2):
        loads[i].start()

    def wait_bytes(ref, sem):
        pltpu.make_async_copy(ref, ref, sem).wait()

    def put(src, dst, send, recv, axis, step):
        pltpu.make_async_remote_copy(
            src_ref=src, dst_ref=dst, send_sem=send, recv_sem=recv,
            device_id={"fsdp": flat(*coord(axis, step))}, device_id_type=MESH,
        ).start()

    def lanes(h, along, other):
        slice_ = flat(*coord(h, along, other))
        first = pair * lax.div(slice_, 2) + wide * lax.rem(slice_, 2)
        return pl.ds(pl.multiple_of(first, 128), main)

    def owned(ref, h, along, other):
        return ref.at[pl.ds(h * unit, unit), lanes(h, along, other)]

    def block(i):
        return pl.ds(i * unit, unit)

    loads[0].wait()
    pl.semaphore_wait(barrier, n_ep + 5)

    for i in (0, 1):
        for h in (0, 1):
            for d, step in ((0, 1), (1, -1)):
                put(owned(down, h, 2, RING[2 * d + i]), down_relay.at[h, d, i],
                    swap_send.at[0], swap_recv.at[2 * h + d], h, step)
    for c in range(4):
        for h in (0, 1):
            for step in (1, -1):
                put(owned(down, h, step, RING[c]), down_ring.at[h, c, block(place(-step))],
                    swap_send.at[0], swap_recv.at[4 + h], h, step)


    n_tok = tok_ref.shape[1]
    tok_ref[feats:] = jnp.zeros((wide - feats, n_tok), BF)
    cot_ref[feats:] = jnp.zeros((wide - feats, n_tok), BF)
    j = lax.broadcasted_iota(jnp.int32, (1, slot), 1)
    index, weight = [], []
    for e in range(n_ep):
        live = j < count_ref[e]
        index.append(jnp.broadcast_to(jnp.where(live, chosen_ref[e : e + 1], -1), (slot, slot)))
        weight.append(jnp.broadcast_to(jnp.where(live, prob_ref[e : e + 1], 0.0), (slot, slot)))
    shape = (rows, slot)
    mine = lax.rem(lax.broadcasted_iota(jnp.int32, shape, 0), slot) == lax.broadcasted_iota(jnp.int32, shape, 1)
    index = jnp.concatenate(index, axis=0).astype(F32)
    index = jnp.sum(jnp.where(mine, index, 0.0), axis=1, keepdims=True).astype(jnp.int32)
    weight = jnp.concatenate(weight, axis=0)
    w_ref[...] = jnp.sum(jnp.where(mine, weight, 0.0), axis=1, keepdims=True)
    hit = lax.broadcasted_iota(jnp.int32, (rows, n_tok), 1) == index
    onehot = jnp.where(hit, 1.0, 0.0).astype(BF)
    hot_ref[...] = onehot

    loads[3].wait()
    loads[4].wait()
    turn_by = lax.rem(wide - 64 * odd, wide)
    gp = pltpu.roll(dot(onehot, cot_ref[...], LAST) * w_ref[...], turn_by, 1)
    tp = pltpu.roll(dot(onehot, tok_ref[...], LAST), turn_by, 1)
    tok_loc[:, :main] = tp[:, :main].astype(BF)
    tok_loc[:, main:] = (tp[:, main:] + pltpu.roll(gp[:, main:], 64, 1)).astype(BF)
    grad_loc[...] = gp[:, :main].astype(BF)

    def scatter(src, dst_of, send, recv, cols=slice(None)):
        @pl.loop(0, n_ep - 1)
        def _(t):
            gap = lax.div(t + 1, 2) * (1 - 2 * lax.rem(t, 2))
            peer = lax.rem(me + n_ep // 2 + gap, n_ep)
            pltpu.make_async_remote_copy(
                src_ref=src.at[pl.ds(peer * slot, slot), cols],
                dst_ref=dst_of(me * slot),
                send_sem=send,
                recv_sem=recv,
                device_id={"ep": peer},
                device_id_type=MESH,
            ).start()

        pltpu.make_async_copy(src.at[pl.ds(me * slot, slot), cols], dst_of(me * slot), recv).start()

    part = lax.div(me, n_ep // 2)
    def lane_half(i):
        return pl.ds(i * (wide // 2), wide // 2)

    for i in (0, 1):
        scatter(tok_loc, lambda r: tok_all.at[f, pl.ds(r, slot), lane_half(i)], a2a_send.at[0],
                a2a_recv.at[2 * part + i], lane_half(i))
    scatter(grad_loc, lambda r: grad_all.at[f, pl.ds(r, slot)], a2a_send.at[1], a2a_recv.at[4])

    def swap_relay():
        for h in (0, 1):
            for d, step in ((0, 1), (1, -1)):
                wait_bytes(down_relay.at[h, d], swap_recv.at[2 * h + d])
                for i in (0, 1):
                    put(down_relay.at[h, d, i], down_ring.at[h, 2 * d + i, block(place(2))],
                        swap_send.at[0], swap_recv.at[4 + h], h, step)

    for h in (0, 1):
        for c in range(4):
            down_ring[h, c, :unit] = down[h * unit : (h + 1) * unit, lanes(h, 0, RING[c])]
    swap_relay()

    def gather(buf, send, g):
        def sem(h, i):
            return ag_recv.at[g * 40 + h * 20 + i]

        def ref(h, fst, snd, q=None):
            o = coord(h, fst, snd)
            first = g * seg + h * piece + (0 if q is None else q * bit)
            return buf.at[flat(*o), pl.ds(first, piece if q is None else bit)]

        def wait(h, i, fst, snd, q=None):
            wait_bytes(ref(h, fst, snd, q), sem(h, i))

        def send_block(h, i, fst, snd, axis, step, q=None):
            r = ref(h, fst, snd, q)
            put(r, r, send, sem(h, i), axis, step)

        def own(h, cols):
            r = ref(h, 0, 0).at[:, cols]
            for i, step in ((0, 1), (1, -1)):
                put(r, r, send, sem(h, i), h, step)
            for i, step in ((4, 1), (5, -1)):
                put(r, r, send, sem(h, i), 1 - h, step)

        def spread(h, j):
            for i, step in ((0, 1), (1, -1)):
                send_block(h, 4 + 4 * j + i, RING[j], 0, 1 - h, step)

        def s1():
            for i in (0, 1):
                o = (-1, 1)[i]
                for h in (0, 1):
                    wait(h, i, o, 0)
                    send_block(h, 2 + i, o, 0, h, -o, i)
                for h in (0, 1):
                    spread(h, 1 + i)

        def relay(j):
            for i in (0, 1):
                o = (-1, 1)[i]
                for h in (1, 0):
                    wait(h, 4 + 4 * j + i, RING[j], o)
                    send_block(h, 6 + 4 * j + i, RING[j], o, 1 - h, -o, i)

        def s3():
            for h in (0, 1):
                wait(h, 2, 2, 0, 0)
                wait(h, 3, 2, 0, 1)
                spread(h, 3)

        def finish():
            for j in range(4):
                for h in (0, 1):
                    for i in (0, 1):
                        wait(h, 6 + 4 * j + i, RING[j], 2, i)

        return own, s1, relay, s3, finish

    def ring(axis, term, land, n, sem, send):
        q1, q2, fp, fm = 0, n, 2 * n, 4 * n

        def init():
            put(term(2, 0), land(q1, n), send, sem(0), axis, 1)
            put(term(2, 1), land(q2, n), send, sem(1), axis, -1)
            put(term(1, 1), land(fp + n, n), send, sem(2), axis, 1)
            put(term(-1, 0), land(fm, n), send, sem(3), axis, -1)

        def comb():
            for i, k, first, dst in ((0, 1, q1, fp), (1, -1, q2, fm + n)):
                r = land(first, n)
                wait_bytes(r, sem(i))
                r[...] = (r[...].astype(F32) + term(k, i)[...].astype(F32)).astype(BF)
                put(r, land(dst, n), send, sem(4 + i), axis, k)

        def total():
            for first, i in ((fp + n, 2), (fm, 3), (fp, 4), (fm + n, 5)):
                wait_bytes(land(first, n), sem(i))
            return (
                term(0)[...].astype(F32)
                + land(fp, 2 * n)[...].astype(F32)
                + land(fm, 2 * n)[...].astype(F32)
            )

        return init, comb, total

    def reduce(buf, in1, in2, res, send, g):
        def make(h, j):
            def term(k, q=None):
                o = coord(h, RING[j], k) if j < 4 else coord(h, k, 0)
                first = g * seg + h * piece + (0 if q is None else q * bit)
                return buf.at[flat(*o), pl.ds(first, piece if q is None else bit)]

            def land(first, n):
                if j < 4:
                    return in1.at[g, h, j, pl.ds(first, n)]
                return in2.at[g, h, pl.ds(first, n)]

            def sem(i):
                return rs_recv.at[g * 60 + h * 30 + j * 6 + i]

            init, comb, total = ring(1 - h if j < 4 else h, term, land, bit, sem, send)

            def fin():
                if j < 4:
                    term(0)[...] = total().astype(BF)
                else:
                    res[pl.ds(g * seg + h * piece, piece)] = total().astype(BF)

            return init, comb, fin

        return {(h, j): make(h, j) for h in (0, 1) for j in range(5)}

    def grad_block(axis, o, q=None):
        g = grad_all.at[flat(*coord(axis, o))]
        return g if q is None else g.at[pl.ds(q * half, half)]

    def grad_sem(axis, i):
        return ag_recv.at[n_seg * 40 + axis * 4 + i]

    tree = [gather(tok_all, ag_send.at[0], g) for g in range(n_seg)]
    own, s1, relay, s3, finish = zip(*tree)
    for i in (0, 1):
        for g in range(n_seg):
            wait_bytes(tok_all.at[f, pl.ds(g * seg, seg), lane_half(i)], a2a_recv.at[2 * g + i])
            for h in (0, 1):
                own[g](h, lane_half(i))
    s1[0]()
    wait_bytes(grad_all.at[f], a2a_recv.at[4])
    for axis in (0, 1):
        for i, step in ((0, 1), (1, -1)):
            put(grad_block(axis, 0), grad_block(axis, 0), ag_send.at[1], grad_sem(axis, i), axis, step)

    def grad_hidden(h):
        wait_bytes(down_ring.at[h, pl.ds(0, 3)], swap_recv.at[4 + h])
        for i in (0, 1):
            wait_bytes(grad_block(1 - h, 2, i), grad_sem(1 - h, 2 + i))
        term = jnp.zeros((4 * unit, rows), F32)
        for c in range(4):
            term = term + dot(down_ring[h, c], grad_block(1 - h, RING[c])[...], LAST)
        gh_own[pl.ds(h * unit, unit)] = term[:unit]
        gh_send[h] = term[unit:].astype(BF)
        for o in (2, 1, -1):
            put(gh_send.at[h, block(place(o) - 1)], gh_in.at[h, place(-o if o < 2 else 2) - 1],
                small_send.at[2 + h], small_recv.at[2 + h], h, o)

    relay[0](0)
    s3[0]()
    for i in (0, 1):
        o = (-1, 1)[i]
        for axis in (0, 1):
            wait_bytes(grad_block(axis, o), grad_sem(axis, i))
            put(grad_block(axis, o, i), grad_block(axis, o, i), ag_send.at[1], grad_sem(axis, 2 + i), axis, -o)
    relay[0](1)
    relay[0](2)
    s1[1]()
    grad_hidden(0)
    relay[0](3)
    n_pair = tok_all.shape[0] // 2
    low = lax.broadcasted_iota(jnp.int32, (seg, 128), 1) < 64

    def span(p, size=pair):
        return pl.ds(pl.multiple_of(p * pair, 128), size)

    def rest(p):
        return pl.ds(pl.multiple_of(p * pair + main, 128), 128)

    def tok_pair(p, r=slice(None)):
        return jnp.concatenate(
            [tok_all[2 * p, r, :main], tok_rem[p, r], tok_all[2 * p + 1, r, :main]], axis=1
        )

    def row_at(d):
        return lax.rem(y + d, SIDE)

    def accumulate(p, g):
        r = pl.ds(g * seg, seg)
        even = tok_all[2 * p, r, main:].astype(F32)
        other = tok_all[2 * p + 1, r, main:].astype(F32)
        tok_rem[p, r] = jnp.where(low, even, other).astype(BF)
        grad_rem[p, r] = pltpu.roll(jnp.where(low, other, even), 64, 1).astype(BF)
        both = jnp.concatenate([gate[span(p)], up[span(p)]], axis=1)
        pre[r] += dot(tok_pair(p, r), both)
        gh_own[:, r] += dot(down[:, rest(p)], grad_rem[p, r], LAST)

    pre[...] = jnp.zeros_like(pre)
    loads[1].wait()
    loads[2].wait()
    relay[1](0)
    grad_hidden(1)
    s3[1]()
    relay[1](1)
    relay[1](2)
    xp = lax.div(x, 2)
    rets = [reduce(ret_part, ret_in, ret_in2, ret_res, rs_send.at[1], g) for g in range(n_seg)]

    def each(g, step, *order):
        for j in order:
            for h in (0, 1):
                rets[g][h, j][step]()

    def forward(g):
        finish[g]()

        @pl.loop(0, n_pair)
        def _(p):
            accumulate(p, g)

    def turn(g):
        r = pl.ds(g * seg, seg)
        pg = pre[r, :128]
        pu = pre[r, 128:]
        sg = jax.nn.sigmoid(pg)
        hid[r] = (pg * sg * pu).astype(BF)
        gh = jnp.transpose(gh_own[:, g * seg : (g + 1) * seg])
        gpre[r, :128] = (gh * pu * sg * (1.0 + pg * (1.0 - sg))).astype(BF)
        gpre[r, 128:] = (gh * (pg * sg)).astype(BF)

    def ret_pair(p, g):
        r = pl.ds(g * seg, seg)
        both = jnp.concatenate([gate[span(p)], up[span(p)]], axis=1)
        t = dot(gpre[r], both, LAST)
        ret_part[2 * p, r, :main] = t[:, :main].astype(BF)
        ret_part[2 * p + 1, r, :main] = t[:, wide:].astype(BF)
        rem = pltpu.roll(t[:, main:wide], 64, 1)
        o = dot(hid[r], down[:, rest(p)])
        ret_part[2 * p, r, main:] = jnp.where(low, o, rem).astype(BF)
        ret_part[2 * p + 1, r, main:] = jnp.where(low, rem, o).astype(BF)

    def back(g):
        @pl.loop(0, 2)
        def _(t):
            ret_pair(2 * row_at(2) + t, g)

        rets[g][1, 3][0]()

        @pl.loop(3, 6)
        def _(t):
            ret_pair(2 * row_at(t) + 1 - xp, g)

        rets[g][0, 3][0]()

        @pl.loop(3, 6)
        def _(t):
            ret_pair(2 * row_at(t) + xp, g)

        each(g, 0, 2, 1, 0)

    forward(0)
    relay[1](3)
    for h in (0, 1):
        wait_bytes(gh_in.at[h], small_recv.at[2 + h])
        gh_own[pl.ds(h * unit, unit)] += (
            gh_in[h, 0].astype(F32) + gh_in[h, 1].astype(F32) + gh_in[h, 2].astype(F32)
        )
    turn(0)
    back(0)
    forward(1)
    turn(1)
    turned = jnp.transpose(hid[...].astype(F32)).astype(BF)
    for h in (0, 1):
        hid_t[h, :unit] = turned[h * unit : (h + 1) * unit]
    for o in (2, 1, -1):
        for h in (0, 1):
            put(hid_t.at[h, block(0)], hid_t.at[h, block(place(-o if o < 2 else 2))],
                small_send.at[h], small_recv.at[h], h, o)
    back(1)
    each(0, 1, 3, 2)

    outs = []
    for h in (0, 1):
        wait_bytes(hid_t.at[h, pl.ds(0, 3 * unit)], small_recv.at[h])
        hid_g[h] = jnp.transpose(hid_t[h].astype(F32)).astype(BF)
        for c in range(4):
            out_part[h, c] = dot(hid_g[h], down_ring[h, c]).astype(BF)

        def term(k, q=None, h=h):
            r = out_part.at[h, place(k)]
            return r if q is None else r.at[pl.ds(q * half, half)]

        def land(first, n, h=h):
            return out_in.at[h, pl.ds(first, n)]

        outs.append(ring(1 - h, term, land, half, lambda i, h=h: out_recv.at[h * 6 + i], rs_send.at[0]))
        outs[h][0]()
    each(0, 1, 1, 0)
    for h in (0, 1):
        outs[h][1]()
    each(1, 1, 3, 2)
    for h in (0, 1):
        for c in range(4):
            gd_part[h, c] = dot(hid_t[h], grad_block(1 - h, RING[c])[...]).astype(BF)
            gdown[h * unit : (h + 1) * unit, lanes(h, 0, RING[c])] = gd_part[h, c, :unit]
    each(0, 2, 3, 2, 1)
    each(0, 0, 4)
    each(1, 1, 1, 0)

    @pl.loop(0, n_pair)
    def _(p):
        g = dot(tok_pair(p), gpre[...], ROWS).astype(BF)
        ggate[span(p)] = g[:, :128]
        gup[span(p)] = g[:, 128:]
        gdown[:, rest(p)] = dot(hid[...], grad_rem[p], ROWS).astype(BF)

    out_res[...] = (outs[0][2]() + outs[1][2]()).astype(BF)
    scatter(out_res, lambda r: out_back.at[pl.ds(r, slot)], back_send.at[0], back_recv.at[0])
    each(0, 1, 4)
    each(1, 2, 3, 2, 1)
    each(1, 0, 4)
    for i in (0, 1):
        for h in (0, 1):
            for d, step in ((0, 1), (1, -1)):
                put(gd_part.at[h, 2 * d + i, block(place(2))], gd_relay.at[h, d, i],
                    swap_send.at[1], swap_recv.at[6 + 2 * h + d], h, step)

    def ret_home(g):
        each(g, 2, 0)
        each(g, 2, 4)
        n_part = n_ep // n_seg
        there = ret_back.at[pl.ds(me * slot, slot)]

        @pl.loop(0, n_part)
        def _(t):
            peer = g * n_part + lax.rem(me + n_part // 2 + t, n_part)

            @pl.when(peer != me)
            def _():
                pltpu.make_async_remote_copy(
                    src_ref=ret_res.at[pl.ds(peer * slot, slot)],
                    dst_ref=there,
                    send_sem=back_send.at[1],
                    recv_sem=back_recv.at[1],
                    device_id={"ep": peer},
                    device_id_type=MESH,
                ).start()

            @pl.when(peer == me)
            def _():
                pltpu.make_async_copy(ret_res.at[pl.ds(me * slot, slot)], there, back_recv.at[1]).start()

    ret_home(0)
    each(1, 1, 4)
    for c in range(4):
        for h in (0, 1):
            for step in (1, -1):
                put(gd_part.at[h, c, block(place(step))], owned(gdown, h, 0, RING[c]),
                    swap_send.at[1], swap_recv.at[10 + h], h, step)
    ret_home(1)
    for h in (0, 1):
        for d, step in ((0, 1), (1, -1)):
            wait_bytes(gd_relay.at[h, d], swap_recv.at[6 + 2 * h + d])
            for i in (0, 1):
                put(gd_relay.at[h, d, i], owned(gdown, h, -step, RING[2 * d + i]),
                    swap_send.at[1], swap_recv.at[10 + h], h, step)

    hot = hot_ref[...]
    body_at = pl.ds(pl.multiple_of(64 * odd, 64), main)
    rest_at = pl.ds(pl.multiple_of(main * (1 - odd), 64), 64)

    def exact(t):
        high = t.astype(BF)
        return dot(high, hot) + dot((t - high.astype(F32)).astype(BF), hot)

    wait_bytes(out_back, back_recv.at[0])
    scaled = jnp.transpose(out_back[...].astype(F32) * w_ref[...])
    mixture_ref[body_at] = exact(scaled).astype(BF)
    wait_bytes(ret_back, back_recv.at[1])
    tail = ret_back[:, main:].astype(F32)
    mix_t[0] = jnp.transpose(tail * w_ref[...])
    mix_t[1] = jnp.transpose(tail)
    back_t = jnp.transpose(ret_back[:, :main].astype(F32)).astype(BF)
    grad_tok_ref[body_at] = dot(back_t, hot).astype(BF)
    mixture_ref[rest_at] = exact(mix_t[0, pl.ds(pl.multiple_of(64 * odd, 64), 64)]).astype(BF)
    piece_t = mix_t[1, pl.ds(pl.multiple_of(64 - 64 * odd, 64), 64)].astype(BF)
    grad_tok_ref[rest_at] = dot(piece_t, hot).astype(BF)

    for h in (0, 1):
        wait_bytes(gd_part.at[h, pl.ds(0, 3)], swap_recv.at[10 + h])
        wait_bytes(hid_t.at[h, pl.ds(0, 3 * unit)], small_send.at[h])
        wait_bytes(gh_send.at[h], small_send.at[2 + h])
    wait_bytes(down_ring, swap_send.at[0])
    wait_bytes(gd_part, swap_send.at[1])
    wait_bytes(tok_loc.at[pl.ds(0, rows - slot)], a2a_send.at[0])
    wait_bytes(grad_loc.at[pl.ds(0, rows - slot)], a2a_send.at[1])
    wait_bytes(tok_all.at[pl.ds(0, 15)], ag_send.at[0])
    wait_bytes(grad_all.at[pl.ds(0, 6)], ag_send.at[1])
    wait_bytes(out_in, rs_send.at[0])
    wait_bytes(ret_part.at[pl.ds(0, 15)], rs_send.at[1])
    wait_bytes(out_res.at[pl.ds(0, rows - slot)], back_send.at[0])
    wait_bytes(ret_res.at[pl.ds(0, rows - slot)], back_send.at[1])


def finish_kernel(*refs):
    n = len(refs) // 2
    stores = [pltpu.make_async_copy(refs[i], refs[n + i], refs[-1].at[i]) for i in range(n)]
    for store in stores:
        store.start()
    for store in stores:
        store.wait()


def per_device(tokens, cotangent, gate_weight, up_weight, down_weight, chosen, counts, gate_prob):
    experts, _, slots = chosen.shape
    n_tok, feats = tokens.shape
    rows = experts * slots
    width = gate_weight.shape[1]
    hidden = gate_weight.shape[2]
    wide, main = 512, 384
    n = width // feats
    vmem = pl.BlockSpec(memory_space=pltpu.VMEM)
    smem = pl.BlockSpec(memory_space=pltpu.SMEM)
    hbm = pl.BlockSpec(memory_space=pl.ANY)
    dma = pltpu.SemaphoreType.DMA
    half = rows // 2
    kept = pl.pallas_call(
        kernel,
        out_shape=(
            pltpu.VMEM((feats, n_tok), BF),
            pltpu.VMEM((feats, n_tok), BF),
            pltpu.VMEM((width, hidden), BF),
            pltpu.VMEM((width, hidden), BF),
            pltpu.VMEM((hidden, width), BF),
        ),
        in_specs=[smem] + [vmem] * 2 + [hbm] * 5,
        out_specs=(vmem,) * 5,
        scratch_shapes=[
            pltpu.VMEM((wide, n_tok), BF),
            pltpu.VMEM((wide, n_tok), BF),
            pltpu.VMEM((rows, main), BF),
            pltpu.VMEM((rows, wide), BF),
            pltpu.VMEM((rows, n_tok), BF),
            pltpu.VMEM((rows, 1), F32),
            pltpu.VMEM((2, wide - main, rows), F32),
            pltpu.VMEM((rows, wide), BF),
            pltpu.VMEM((rows, main), BF),
            pltpu.VMEM((n, rows, wide), BF),
            pltpu.VMEM((n, rows, main), BF),
            pltpu.VMEM((n // 2, rows, 128), BF),
            pltpu.VMEM((n // 2, rows, 128), BF),
            pltpu.VMEM((width, hidden), BF),
            pltpu.VMEM((width, hidden), BF),
            pltpu.VMEM((hidden, width), BF),
            pltpu.VMEM((2, 4, 256, main), BF),
            pltpu.VMEM((2, 2, 2, 64, main), BF),
            pltpu.VMEM((2, 4, 256, main), BF),
            pltpu.VMEM((2, 2, 2, 64, main), BF),
            pltpu.VMEM((rows, hidden), BF),
            pltpu.VMEM((2, 256, rows), BF),
            pltpu.VMEM((2, rows, 256), BF),
            pltpu.VMEM((2, 192, rows), BF),
            pltpu.VMEM((hidden, rows), F32),
            pltpu.VMEM((2, 3, 64, rows), BF),
            pltpu.VMEM((rows, 2 * hidden), F32),
            pltpu.VMEM((rows, 2 * hidden), BF),
            pltpu.VMEM((2, 4, rows, main), BF),
            pltpu.VMEM((n, rows, wide), BF),
            pltpu.VMEM((2, 3 * rows, main), BF),
            pltpu.VMEM((2, 2, 4, 3 * half // 2, wide), BF),
            pltpu.VMEM((2, 2, 3 * half // 2, wide), BF),
            pltpu.VMEM((rows, main), BF),
            pltpu.VMEM((rows, wide), BF),
            dma((5,)),
            dma((2,)),
            dma((5,)),
            dma((2,)),
            dma((88,)),
            dma((2,)),
            dma((120,)),
            dma((12,)),
            dma((2,)),
            dma((2,)),
            dma((2,)),
            dma((12,)),
            dma((4,)),
            dma((4,)),
        ],
        compiler_params=pltpu.CompilerParams(
            collective_id=0, has_side_effects=True, vmem_limit_bytes=52 * 1024 * 1024
        ),
        name="experts",
    )(
        counts[:, 0],
        chosen[:, 0, :],
        gate_prob[:, 0, :],
        tokens.T,
        cotangent.T,
        gate_weight[0],
        up_weight[0],
        down_weight[0],
    )
    mixture, grad_tokens, grad_gate, grad_up, grad_down = pl.pallas_call(
        finish_kernel,
        out_shape=(
            jax.ShapeDtypeStruct((feats, n_tok), BF),
            jax.ShapeDtypeStruct((feats, n_tok), BF),
            jax.ShapeDtypeStruct((width, hidden), BF),
            jax.ShapeDtypeStruct((width, hidden), BF),
            jax.ShapeDtypeStruct((hidden, width), BF),
        ),
        in_specs=[vmem] * 5,
        out_specs=(hbm,) * 5,
        scratch_shapes=[dma((5,))],
        compiler_params=pltpu.CompilerParams(vmem_limit_bytes=16 * 1024 * 1024),
        name="finish",
    )(*kept)
    return mixture.T, grad_tokens.T, grad_gate[None], grad_up[None], grad_down[None]


def solution(mesh):
    placed = (
        P("ep", "fsdp"),
        P("ep", "fsdp"),
        P("ep", None, "fsdp"),
        P("ep", None, "fsdp"),
        P("ep", "fsdp", None),
        P(None, "ep", None),
        P(None, "ep"),
        P(None, "ep", None),
    )
    return jax.shard_map(
        per_device,
        mesh=mesh,
        in_specs=placed,
        out_specs=(
            P("ep", "fsdp"),
            P("ep", "fsdp"),
            P("ep", None, "fsdp"),
            P("ep", None, "fsdp"),
            P("ep", "fsdp", None),
        ),
        check_vma=False,
    )
```
